256 devices in a mesh: flow: 32 (over y, x, core), span: 8 (over z).
Axes of the slice: x: 4, y: 4, z: 8, core: 2. Of those that a mesh axis runs over, the one named last changes fastest.
Arguments:
- solid_start: float32 [32, 2048, 1024], P(None, 'flow', 'span'), may hold values from -6 to 6
- heat_gen: float32 [32, 2048, 1024], P(None, 'flow', 'span'), may hold values from 0 to 0.05
- conductance: float32 [128, 65536], P('span', 'flow'), may hold values from 0 to 1, as said below
- heat_capacity: float32 [128], P('span'), may hold values from 0.2 to 1
- inlet_temp: float32 [128], P('span'), may hold values from -4 to 4
- wall_owner: int32 [65536, 1], P(('flow', 'span')), may hold values from 0 to 31; in each aligned block of 256 rows (0 to 255, 256 to 511, ...) at most 16 rows name the same one
- wall_row: int32 [65536, 1], P(('flow', 'span')), may hold values from 0 to 63
Outputs:
- solid_final: float32 [32, 2048, 1024], P(None, 'flow', 'span')
- coolant_final: float32 [128, 65536], P('span', 'flow')
The draws below stay inside these ranges and needn't reach their ends.
Inputs may be any that keep to these rules, and one draw needn't show every extreme that they name: `conductance`: Positive. `wall_owner`: within the segments of one device (aligned blocks of 256 rows) no flow index is named more than 16 times, and some flow index is named exactly 16 times.
All inputs are finite; a program needn't handle non-finite values.
Results may differ from the reference program's by a relative error of at most 0.0003.
Values sent between devices are 32-bit elements; how exact they have to be, the bound alone decides.
No kernel may reach another device: no remote copies, remote signals or barrier semaphores. Data moves between devices by JAX's collectives and lax.ppermute only.
A program may use at most 128 MiB of HBM per device.

```python
import math
import jax
import jax.numpy as jnp
import numpy as np
from jax import lax

SEG = 128
NZ = 32
CX = 64
CH_DEV = 16
ST_DEV = 2048
STEPS = 10
NX = 2048
NY = 1024
CHANNELS = 128
CHANNEL_STATIONS = 65536
SEG_DEV = 256
SEGS = 65536
CAP = 16
N_FLOW = 32
N_SPAN = 8


def draw_conductance(key, part):
    random_child_keys = jax.random.split(key, 6)
    solid_grid_shape = (CHANNELS, CHANNEL_STATIONS)
    fast_share = 0.5
    fast_mask = jax.random.uniform(random_child_keys[0], (CHANNELS, 1)) < fast_share
    slow_rates = jnp.exp(jax.random.uniform(random_child_keys[1], (CHANNELS, 1), jnp.float32, math.log(5.0), math.log(40.0))) / CHANNEL_STATIONS
    fast_rates = jnp.exp(jax.random.uniform(random_child_keys[2], (CHANNELS, 1), jnp.float32, math.log(1.0 / 50.0), math.log(1.0 / 30.0)))
    decay_rates = jnp.where(fast_mask, fast_rates, slow_rates)
    surface_texture = jax.random.uniform(random_child_keys[3], solid_grid_shape, jnp.float32, 0.5, 1.5)
    surge_event_mask = jax.random.uniform(random_child_keys[4], solid_grid_shape) < 3.0 / CHANNEL_STATIONS
    surge_heat_loss = jax.random.uniform(random_child_keys[5], solid_grid_shape, jnp.float32, 0.2, 0.5)
    sampled_values = jnp.where(surge_event_mask, -jnp.log(1.0 - surge_heat_loss), decay_rates * surface_texture)
    return sampled_values.astype(jnp.float32)


def set_ends(array, rng, low, largest):
    shape = array.shape
    place = [jax.random.randint(jax.random.fold_in(rng, axis), (), 0, shape[axis]) for axis in range(len(shape))]
    array = array.at[tuple(place)].set(low)
    longest = shape.index(max(shape))
    place[longest] = (place[longest] + 1) % shape[longest]
    return array.at[tuple(place)].set(largest)


def block_scale(own_key, extent, cuts, least, top_value):
    gain, own = 1.0, jax.random.fold_in(own_key, 6)
    for axis_at, shards_of in cuts:
        heights = jnp.exp(jax.random.uniform(jax.random.fold_in(own, axis_at), (shards_of,), jnp.float32, least / len(cuts), top_value / len(cuts)))
        gain = gain * jnp.repeat(heights, extent[axis_at] // shards_of).reshape([-1 if axis == axis_at else 1 for axis in range(len(extent))])
    return gain


def deal_out(own_key, own, number, rows, amount, top, reach, skew):
    sequence = jax.random.permutation(own_key, amount)
    crowded, common = portions_of(amount, rows * top, reach, skew, True), portions_of(amount, rows * top, reach, skew, False)
    places = jnp.arange(amount)

    def named(sizes, rotation):
        used = int((sizes > 0).sum())
        fixed = max(1, used // 4)
        shifted = fixed + (places - fixed + rotation * (used - fixed)) % max(1, amount - fixed)
        return jnp.zeros((amount,), jnp.int32).at[sequence[jnp.where(places < fixed, places, shifted)]].set(jnp.asarray(sizes, jnp.int32))

    sizes = jnp.where(number % 4 == 0, named(crowded, number // 4), named(common, number - number // 4 - 1))
    mixed = jax.random.permutation(jax.random.fold_in(own, 3), amount)
    giver, receiver = mixed[0:amount // 2 * 2:2], mixed[1:amount // 2 * 2:2]
    margin = jnp.minimum(sizes[giver] - 1, reach - sizes[receiver]) // 2
    margin = jnp.where((giver == sequence[0]) | (receiver == sequence[0]) | (sizes[receiver] == 0), 0, jnp.maximum(margin, 0))
    shifted = jax.random.randint(jax.random.fold_in(own, 4), (amount // 2,), 0, 1 << 20) % (margin + 1)
    sizes = sizes.at[giver].add(-shifted).at[receiver].add(shifted)
    labels = jnp.searchsorted(jnp.cumsum(sizes), jnp.arange(rows * top), side="right").astype(jnp.int32)
    table = labels.reshape(top, rows).T
    table = table[jax.random.permutation(jax.random.fold_in(own, 1), rows)]
    rotation = jax.random.randint(jax.random.fold_in(own, 2), (rows, 1), 0, top)
    return jnp.take_along_axis(table, (jnp.arange(top)[None, :] + rotation) % top, axis=1)


def portions_of(count, total, most, lean, full):
    portions = [(1 << 20) // math.isqrt(grade ** lean) + 1 for grade in range(1, count + 1)]
    largest = most if full else min(most, max(-(-total // count), total * portions[0] // sum(portions)))
    least = 1 if total - largest >= count - 1 else 0
    given, rest = [largest] + [least] * (count - 1), total - largest - least * (count - 1)
    while rest > 0:
        free = [i for i in range(1, count) if given[i] < largest] or [i for i in range(1, count) if given[i] < most]
        pool, budget = sum([portions[i] for i in free]), rest
        for i in free:
            extra = min(most - given[i], max(1, budget * portions[i] // pool), rest)
            given[i] = given[i] + extra
            rest = rest - extra
    return np.array(given)


def noise(own_key, dims, scale, most, shards=(), kind=jnp.bfloat16):
    level = block_scale(own_key, dims, shards, -0.22, 0.18) if shards else 1.0
    array = jax.random.normal(own_key, dims, jnp.float32) * scale * level
    return jnp.minimum(jnp.maximum(array, -most), most).astype(kind)


def setup_inputs(seed: int = 0) -> dict:
    seeds = jax.random.split(jax.random.key(seed), 8)
    solid_start = noise(seeds[0], (NZ, NX, NY), 1.0, 6.0, ((1, 32), (2, 8)), jnp.float32)
    heat_gen = jnp.clip(0.05 * jax.random.uniform(seeds[1], (NZ, NX, NY), jnp.float32) ** block_scale(seeds[1], (NZ, NX, NY), ((1, 32), (2, 8)), -0.2, 0.2), 0.0, 0.05)
    conductance = draw_conductance(jax.random.fold_in(seeds[7], 71), 0)
    heat_capacity = jnp.clip(jnp.exp(math.log(1.0) - 1.609438 * jax.random.uniform(seeds[3], (CHANNELS,), jnp.float32) ** block_scale(seeds[3], (CHANNELS,), ((0, 8),), -0.2, 0.2)), 0.2, 1.0)
    inlet_temp = noise(seeds[4], (CHANNELS,), 1.0, 4.0, ((0, 8),), jnp.float32)
    wall_owner_keys = jax.random.split(jax.random.fold_in(seeds[5], 1), SEGS // SEG_DEV)
    wall_owner_turns = jax.random.permutation(jax.random.fold_in(seeds[5], 3), SEGS // SEG_DEV)
    wall_owner = jax.vmap(lambda own, number: deal_out(jax.random.fold_in(seeds[5], 2), own, number, SEG_DEV, N_FLOW, 1, CAP, 2))(wall_owner_keys, wall_owner_turns).reshape((SEGS, 1))
    wall_row = set_ends(jax.random.randint(seeds[6], (SEGS, 1), 0, CX), jax.random.fold_in(seeds[6], 1), 0, CX - 1).astype(jnp.int32)
    return {"solid_start": solid_start, "heat_gen": heat_gen, "conductance": conductance, "heat_capacity": heat_capacity, "inlet_temp": inlet_temp, "wall_owner": wall_owner, "wall_row": wall_row}


KAPPA = 0.16


def compose(earlier, later):
    return (earlier[0] * later[0], later[0] * earlier[1] + later[1])


def regroup(sampled_values, seg_count):
    sampled_values = sampled_values.reshape(N_FLOW, N_SPAN, CH_DEV, seg_count)
    return jnp.transpose(sampled_values, (1, 2, 0, 3)).reshape(CHANNELS, N_FLOW * seg_count)


def conduct(field, heat_gen):
    padded = jnp.pad(field, 1)
    beside = padded[2:, 1:-1, 1:-1] + padded[:-2, 1:-1, 1:-1]
    beside = beside + padded[1:-1, 2:, 1:-1] + padded[1:-1, :-2, 1:-1]
    beside = beside + padded[1:-1, 1:-1, 2:] + padded[1:-1, 1:-1, :-2]
    return field + KAPPA * (beside - 6.0 * field) + heat_gen


def reference(solid_start, heat_gen, conductance, heat_capacity, inlet_temp, wall_owner, wall_row):
    seg_count = ST_DEV // SEG
    wall_cell = regroup(wall_owner[:, 0], seg_count) * CX + regroup(wall_row[:, 0], seg_count)
    wall_cell = wall_cell.astype(jnp.int32)
    span_band = (jnp.arange(CHANNELS, dtype=jnp.int32) // CH_DEV).astype(jnp.int32)[:, None]
    decays = jnp.exp(-conductance)
    solid_field = solid_start
    coolant = jnp.zeros((CHANNELS, CHANNEL_STATIONS), jnp.float32)
    for turn in range(STEPS):
        bottom_layer = solid_field[0].reshape(NX, N_SPAN, SEG)
        wall_temp = bottom_layer[wall_cell, span_band].reshape(CHANNELS, CHANNEL_STATIONS)
        gain_pre, shift_pre = lax.associative_scan(compose, (decays, (1.0 - decays) * wall_temp), axis=1)
        coolant = gain_pre * inlet_temp[:, None] + shift_pre
        upstream = jnp.concatenate([inlet_temp[:, None], coolant[:, :-1]], axis=1)
        heat_flow = heat_capacity[:, None] * (coolant - upstream)
        wall_sink = jnp.zeros((NX, N_SPAN, SEG), jnp.float32)
        wall_sink = wall_sink.at[wall_cell, span_band].add(heat_flow.reshape(CHANNELS, N_FLOW * seg_count, SEG))
        solid_field = conduct(solid_field, heat_gen)
        solid_field = solid_field.at[0].add(-wall_sink.reshape(NX, NY))
    return solid_field, coolant
```

```python
import functools

import jax
import jax.numpy as jnp
from jax import lax
from jax.experimental import pallas as pl
from jax.experimental.pallas import tpu as pltpu
from jax.sharding import PartitionSpec as P

STEPS = 10
KAPPA = 0.16
F32 = jnp.float32
I32 = jnp.int32
HI = lax.Precision.HIGHEST
LANES = 128
SLOTS = 16
VMEM_LIMIT = 24 << 20


def iota(shape, dim):
    return lax.broadcasted_iota(I32, shape, dim)


def dot(a, b):
    return jnp.dot(a, b, precision=HI, preferred_element_type=F32)


def dot_t(a, b):
    return lax.dot_general(
        a, b, (((1,), (1,)), ((), ())), precision=HI, preferred_element_type=F32
    )


def pick(values, index):
    return jnp.take_along_axis(values, index, axis=1, mode="promise_in_bounds")


def call(kernel, out_shape, n_in, smem=(), flops=0, nbytes=0, **kw):
    return pl.pallas_call(
        kernel,
        out_shape=out_shape,
        in_specs=[
            pl.BlockSpec(memory_space=pltpu.SMEM if k in smem else pltpu.VMEM) for k in range(n_in)
        ],
        out_specs=jax.tree.map(lambda _: pl.BlockSpec(memory_space=pltpu.VMEM), out_shape),
        compiler_params=pltpu.CompilerParams(vmem_limit_bytes=VMEM_LIMIT),
        cost_estimate=pl.CostEstimate(flops=flops, bytes_accessed=nbytes, transcendentals=0),
        **kw,
    )


def shape(*dims):
    return jax.ShapeDtypeStruct(dims, F32)


def ishape(*dims):
    return jax.ShapeDtypeStruct(dims, I32)


def source_kernel(owner_ref, row_ref, cond_ref, pay_ref, place_ref):
    segs = cond_ref.shape[0]
    n_flow = pay_ref.shape[0]
    cond = cond_ref[...]
    own_col = jnp.broadcast_to(owner_ref[...], (segs, segs))
    sub, lane = iota((segs, segs), 0), iota((segs, segs), 1)
    own_row = jnp.sum(jnp.where(sub == lane, own_col, 0), axis=0, keepdims=True)
    same = own_col == own_row
    rank_row = jnp.sum((same & (sub < lane)).astype(F32), axis=0, keepdims=True).astype(I32)
    rank_col = jnp.sum((same & (lane < sub)).astype(F32), axis=1, keepdims=True).astype(I32)
    slot_row = own_row * SLOTS + rank_row
    slot_col = owner_ref[...] * SLOTS + rank_col
    slots = n_flow * SLOTS
    chosen = (iota((slots, segs), 0) == slot_row).astype(F32)
    moved = dot(chosen, cond)
    lanes = iota((segs, LANES), 1)
    value = jnp.where(lanes < SLOTS, row_ref[...], iota((segs, LANES), 0))
    value = jnp.where((lanes < 2 * SLOTS) & (lanes % SLOTS == rank_col), value, 0).astype(F32)
    held = (iota((n_flow, segs), 0) == own_row).astype(F32)
    meta = dot(held, value)
    total = dot_t(jnp.ones((8, LANES), F32), cond)[0:1]
    sub8 = iota((8, LANES), 0)
    common = jnp.zeros((8, LANES), F32)
    slot_f = slot_row.astype(F32)
    for half in range(2):
        cols = slice(half * LANES, (half + 1) * LANES)
        common = jnp.where(sub8 == 1 + half, slot_f[:, cols], common)
        common = jnp.where(sub8 == 3 + half, total[:, cols], common)
    for p in range(n_flow):
        pay_ref[p, 0:SLOTS, :] = moved[p * SLOTS : (p + 1) * SLOTS]
        pay_ref[p, SLOTS : SLOTS + 8, :] = jnp.where(sub8 == 0, meta[p : p + 1], common)
    place_ref[...] = (iota((segs, slots), 1) == slot_col).astype(F32)


def owner_kernel(
    got_ref, bottom_ref, cap_ref,
    hit_ref, hitcap_ref, hit_t_ref, rate_ref, reply_ref, weight_t_ref, level_ref,
    lane_ref, from_ref, seg_ref, hop_ref, behind_ref, pick_ref, msg_ref,
):
    n_flow = got_ref.shape[0]
    slots = n_flow * SLOTS
    cond = got_ref[:, 0:SLOTS, :].reshape(slots, LANES)
    lane = iota((slots, LANES), 1)
    decay = jnp.exp(-cond)
    rate = 1.0 - decay
    rate_ref[...] = rate
    sub_t, lane_t = iota((LANES, LANES), 0), iota((LANES, LANES), 1)
    ahead = dot(cond, (sub_t < lane_t).astype(F32))
    after = dot(cond, (sub_t > lane_t).astype(F32))
    reply_ref[...] = rate * jnp.exp(-ahead)
    weight_t = jnp.transpose(rate * jnp.exp(-after))
    weight_t_ref[...] = weight_t
    gain = decay
    for level in range(7):
        step = 1 << level
        level_ref[level] = jnp.where(lane >= step, gain, 0.0)
        if level < 6:
            gain = gain * jnp.where(lane >= step, pltpu.roll(gain, step, 1), 1.0)
    meta = got_ref[:, SLOTS, :]
    lane8, sub8 = iota((8, LANES), 1), iota((8, LANES), 0)
    mine = lane8 // SLOTS == sub8
    hits, caps = [], []
    n_grp = n_flow // 8
    rows = iota((LANES, LANES), 0)
    for g in range(n_grp):
        part = meta[g * 8 : g * 8 + 8]
        row = jnp.sum(jnp.where(mine, pick(part, lane8 % SLOTS), 0.0), axis=0, keepdims=True)
        seg = jnp.sum(
            jnp.where(mine, pick(part, SLOTS + lane8 % SLOTS), 0.0), axis=0, keepdims=True
        )
        seg = seg.astype(I32)
        pick_ref[g * 8 : g * 8 + 8, :] = jnp.broadcast_to(seg, (8, LANES))
        cap = pick(
            jnp.broadcast_to(cap_ref[...], (8, LANES)), jnp.broadcast_to(seg // 16, (8, LANES))
        )[0:1]
        hits.append((rows == row.astype(I32)).astype(F32))
        caps.append(cap)
    hit = jnp.concatenate(hits, axis=1)
    hit_t_ref[...] = jnp.transpose(hit)
    block_rows = bottom_ref.shape[0]
    hit = hit[0:block_rows]
    hit_ref[...] = hit
    hitcap_ref[...] = hit * jnp.concatenate(caps, axis=1)
    lane_f, sub_f = iota((n_flow, LANES), 1), iota((n_flow, LANES), 0)
    for half in range(2):
        slot = got_ref[:, SLOTS + 1 + half, :].astype(I32)
        from_ref[half] = slot // SLOTS
        lane_ref[half] = (sub_f % 8) * SLOTS + slot % SLOTS
        gain = jnp.exp(-got_ref[:, SLOTS + 3 + half, :])
        inner = lane_f % 16
        for level in range(4):
            step = 1 << level
            seg_ref[level, half] = jnp.where(inner >= step, gain, 0.0)
            gain = gain * jnp.where(inner >= step, pltpu.roll(gain, step, 1), 1.0)
        behind_ref[half] = jnp.where(inner == 0, 1.0, pltpu.roll(gain, 1, 1))
        hop_ref[5, half] = gain
        for level in range(5):
            step = 1 << level
            hop_ref[level, half] = jnp.where(sub_f >= step, gain, 0.0)
            gain = gain * jnp.where(sub_f >= step, pltpu.roll(gain, step, 0), 1.0)
    write_shifts(bottom_ref[...], weight_t, hit, msg_ref, 0)


def write_shifts(bottom, weight_t, hit, msg_ref, at):
    ends = jnp.sum(dot(bottom, weight_t) * hit, axis=0, keepdims=True)
    sub8 = iota((8, LANES), 0)
    tile = jnp.zeros((8, LANES), F32)
    for g in range(ends.shape[1] // LANES):
        tile = jnp.where(sub8 == g, ends[:, g * LANES : (g + 1) * LANES], tile)
    for p in range(msg_ref.shape[0]):
        msg_ref[p, at : at + 8, :] = tile


def march(temp, rate, level_ref):
    shift = rate * temp
    for level in range(7):
        shift = shift + level_ref[level] * pltpu.roll(shift, 1 << level, 1)
    return shift


def beside_kernel(
    edge_ref, solid_ref, bottom_ref, heat_ref, west_ref, east_ref, north_ref, south_ref,
    hit_t_ref, rate_ref, level_ref, hitcap_ref,
    out_ref, base_ref, cols_ref, head_ref, tail_ref,
):
    nz, nx, ny = solid_ref.shape
    lane = iota((nx, ny), 1)
    sub = iota((nx, ny), 0)
    border = (lane == 0) | (lane == ny - 1)
    cols_in = jnp.where(
        lane < nz, east_ref[...] * edge_ref[1], west_ref[...] * edge_ref[0]
    )
    north_on, south_on = edge_ref[2], edge_ref[3]

    def layer(z, mid, low, high, cols):
        side = jnp.where(lane == 0, nz, 0) + z
        halo = pick(cols_in, side)
        right, left = pltpu.roll(mid, 1, 1), pltpu.roll(mid, ny - 1, 1)
        across = jnp.where(border, halo, right) + jnp.where(
            border, jnp.where(lane == 0, left, right), left
        )
        up = jnp.where(sub == 0, north_ref[pl.ds(z, 1), :] * north_on, pltpu.roll(mid, 1, 0))
        down = jnp.where(
            sub == nx - 1, south_ref[pl.ds(z, 1), :] * south_on, pltpu.roll(mid, nx - 1, 0)
        )
        total = across + (up + down)
        if low is not None:
            total = total + low
        if high is not None:
            total = total + high
        new = mid + KAPPA * (total - 6.0 * mid) + heat_ref[z]
        return new

    def keep(z, new, cols):
        out_ref[z] = new
        head_ref[pl.ds(z, 1), :] = new[0:1]
        tail_ref[pl.ds(z, 1), :] = new[nx - 1 : nx]
        ends = pick(new, jnp.where(lane < nz, 0, ny - 1))
        return jnp.where(lane % nz == z, ends, cols)

    bottom = bottom_ref[...]
    base = layer(0, bottom, None, solid_ref[1], None)
    head_ref[0:1, :] = base[0:1]
    tail_ref[0:1, :] = base[0:1]
    cols = jnp.zeros((nx, ny), F32)
    cols = keep(1, layer(1, solid_ref[1], bottom, solid_ref[2], cols), cols)

    def body(z, cols):
        return keep(
            z, layer(z, solid_ref[z], solid_ref[z - 1], solid_ref[z + 1], cols), cols
        )

    cols = lax.fori_loop(2, nz - 1, body, cols)
    cols = keep(nz - 1, layer(nz - 1, solid_ref[nz - 1], solid_ref[nz - 2], None, cols), cols)
    cols_ref[...] = cols
    padded = jnp.concatenate([bottom, jnp.zeros((LANES - nx, ny), F32)], axis=0)
    temp = dot(hit_t_ref[...], padded)
    rate = rate_ref[...]
    shift = march(temp, rate, level_ref)
    before = jnp.where(iota(shift.shape, 1) == 0, 0.0, pltpu.roll(shift, 1, 1))
    base_ref[...] = base - dot(hitcap_ref[...], rate * (temp - before))


def entering(got_ref, at, inlet_ref, lane_ref, from_ref, seg_ref, hop_ref, behind_ref):
    n_flow = got_ref.shape[0]
    n_grp = n_flow // 8
    ends = [[], []]
    for g in range(n_grp):
        rows = slice(g * 8, g * 8 + 8)
        index = [lane_ref[half, rows, :] for half in range(2)]
        source = [from_ref[half, rows, :] for half in range(2)]
        acc = [jnp.zeros((8, LANES), F32) for _ in range(2)]
        for o in range(n_flow):
            line = jnp.broadcast_to(got_ref[o, at + g : at + g + 1, :], (8, LANES))
            for half in range(2):
                acc[half] = jnp.where(source[half] == o, pick(line, index[half]), acc[half])
        for half in range(2):
            ends[half].append(acc[half])
    result = []
    sub, lane = iota((n_flow, LANES), 0), iota((n_flow, LANES), 1)
    for half in range(2):
        x = jnp.concatenate(ends[half], axis=0)
        for level in range(4):
            x = x + seg_ref[level, half] * pltpu.roll(x, 1 << level, 1)
        inlet = inlet_ref[half]
        y = jnp.where(sub == 0, x + hop_ref[5, half] * inlet, x)
        for level in range(5):
            y = y + hop_ref[level, half] * pltpu.roll(y, 1 << level, 0)
        carry = jnp.where(sub == 0, inlet, pltpu.roll(y, 1, 0))
        carry = pick(carry, lane // 16 * 16 + 15)
        earlier = jnp.where(lane % 16 == 0, 0.0, pltpu.roll(x, 1, 1))
        result.append(earlier + behind_ref[half] * carry)
    return result


def hosted(enter, pick_ref):
    n_grp = enter[0].shape[0] // 8
    lane8, sub8 = iota((8, LANES), 1), iota((8, LANES), 0)
    parts = []
    for g in range(n_grp):
        seg = pick_ref[g * 8 : g * 8 + 8, :]
        rows = slice(g * 8, g * 8 + 8)
        low, high = (pick(enter[half][rows], seg % LANES) for half in range(2))
        found = jnp.where(seg < LANES, low, high)
        found = jnp.where(lane8 // SLOTS == sub8, found, 0.0)
        parts.append(jnp.sum(found, axis=0, keepdims=True))
    return jnp.concatenate(parts, axis=1)


def after_kernel(
    last,
    got_ref, base_ref, cols_in_ref, head_in_ref, tail_in_ref, inlet_ref,
    lane_ref, from_ref, seg_ref, hop_ref, behind_ref, pick_ref,
    hit_ref, hitcap_ref, reply_ref, weight_t_ref, hit_t_ref,
    bottom_ref, msg_ref, cols_ref, head_ref, tail_ref,
):
    enter = entering(got_ref, 0, inlet_ref, lane_ref, from_ref, seg_ref, hop_ref, behind_ref)
    carry = hosted(enter, pick_ref)
    bottom = base_ref[...] + dot(hitcap_ref[...] * carry, reply_ref[...])
    bottom_ref[...] = bottom
    nx, ny = bottom.shape
    nz = head_ref.shape[0]
    lane = iota((nx, ny), 1)
    ends = pick(bottom, jnp.where(lane < nz, 0, ny - 1))
    cols_ref[...] = jnp.where(lane % nz == 0, ends, cols_in_ref[...])
    sub = iota((nz, ny), 0)
    head_ref[...] = jnp.where(sub == 0, bottom[0:1], head_in_ref[...])
    tail_ref[...] = jnp.where(sub == 0, bottom[nx - 1 : nx], tail_in_ref[...])
    if last:
        padded = jnp.concatenate([bottom, jnp.zeros((LANES - nx, ny), F32)], axis=0)
        temp = dot(hit_t_ref[...], padded)
        for p in range(msg_ref.shape[0]):
            msg_ref[p, 8 : 8 + SLOTS, :] = temp[p * SLOTS : (p + 1) * SLOTS]
    write_shifts(bottom, weight_t_ref[...], hit_ref[...], msg_ref, 0)


def final_kernel(
    me_ref, got_ref, base_ref, inlet_ref,
    lane_ref, from_ref, seg_ref, hop_ref, behind_ref, pick_ref,
    hitcap_ref, reply_ref, place_ref, cond_ref,
    bottom_ref, coolant_ref,
):
    enter = entering(got_ref, 0, inlet_ref, lane_ref, from_ref, seg_ref, hop_ref, behind_ref)
    carry = hosted(enter, pick_ref)
    bottom_ref[...] = base_ref[...] + dot(hitcap_ref[...] * carry, reply_ref[...])
    n_flow = got_ref.shape[0]
    temp = dot(place_ref[...], got_ref[:, 8 : 8 + SLOTS, :].reshape(n_flow * SLOTS, LANES))
    segs = temp.shape[0]
    lane = iota((segs, LANES), 1)
    gain = jnp.exp(-cond_ref[...])
    shift = (1.0 - gain) * temp
    for level in range(7):
        step = 1 << level
        shift = shift + jnp.where(lane >= step, gain * pltpu.roll(shift, step, 1), 0.0)
        gain = gain * jnp.where(lane >= step, pltpu.roll(gain, step, 1), 1.0)
    own = iota((n_flow, LANES), 0) == me_ref[0]
    line = jnp.concatenate(
        [jnp.sum(jnp.where(own, part, 0.0), axis=0, keepdims=True) for part in enter], axis=1
    )
    same = iota((segs, segs), 0) == iota((segs, segs), 1)
    start = jnp.sum(jnp.where(same, line, 0.0), axis=1, keepdims=True)
    coolant_ref[...] = shift + gain * start


def body(solid_start, heat_gen, conductance, heat_capacity, inlet_temp, wall_owner, wall_row):
    n_flow, n_span = lax.axis_size("flow"), lax.axis_size("span")
    me, lot = lax.axis_index("flow"), lax.axis_index("span")
    nz, nx, ny = solid_start.shape
    channels, stations = conductance.shape
    segs = wall_owner.shape[0]
    slots = n_flow * SLOTS
    cond = conductance.reshape(segs, LANES)
    edge = jnp.stack([lot > 0, lot < n_span - 1, me > 0, me < n_flow - 1]).astype(F32)
    me1 = me.astype(I32).reshape(1)
    cap = jnp.pad(heat_capacity.reshape(1, channels), ((0, 0), (0, LANES - channels)))
    inlet = jnp.repeat(inlet_temp, segs // channels).reshape(2, 1, LANES)

    def beside_span(cols):
        ahead = [(i, (i + 1) % n_span) for i in range(n_span)]
        back = [(i, (i - 1) % n_span) for i in range(n_span)]
        return lax.ppermute(cols, "span", ahead), lax.ppermute(cols, "span", back)

    def beside_flow(head, tail):
        ahead = [(i, (i + 1) % n_flow) for i in range(n_flow)]
        back = [(i, (i - 1) % n_flow) for i in range(n_flow)]
        return lax.ppermute(tail, "flow", ahead), lax.ppermute(head, "flow", back)

    def exchange(message):
        return lax.all_to_all(message, "flow", 0, 0, tiled=True)

    pay, place = call(
        source_kernel, (shape(n_flow, SLOTS + 8, LANES), shape(segs, slots)), 3
    )(wall_owner, wall_row, cond)
    got = exchange(pay)
    cols = jnp.pad(
        jnp.concatenate([solid_start[:, :, 0].T, solid_start[:, :, ny - 1].T], axis=1),
        ((0, 0), (0, LANES - 2 * nz)),
    )
    head, tail = solid_start[:, 0, :], solid_start[:, nx - 1, :]
    bottom = solid_start[0]
    (
        hit, hitcap, hit_t, rate, reply, weight_t, level,
        lanes, origin, seg, hop, behind, chosen, message,
    ) = call(
        owner_kernel,
        (
            shape(nx, slots), shape(nx, slots), shape(slots, LANES), shape(slots, LANES),
            shape(slots, LANES), shape(LANES, slots), shape(7, slots, LANES),
            ishape(2, n_flow, LANES), ishape(2, n_flow, LANES), shape(4, 2, n_flow, LANES),
            shape(6, 2, n_flow, LANES), shape(2, n_flow, LANES), ishape(n_flow, LANES),
            shape(n_flow, 8, LANES),
        ),
        3,
    )(got, bottom, cap)
    scan = (lanes, origin, seg, hop, behind, chosen)
    solid = solid_start
    for turn in range(STEPS):
        west, east = beside_span(cols)
        north, south = beside_flow(head, tail)
        got = exchange(message)
        solid, base, cols, head, tail = call(
            beside_kernel,
            (shape(nz, nx, ny), shape(nx, ny), shape(nx, ny), shape(nz, ny), shape(nz, ny)),
            12,
            smem=(0,),
            flops=20_000_000,
            nbytes=6_000_000,
        )(edge, solid, bottom, heat_gen, west, east, north, south, hit_t, rate, level, hitcap)
        if turn < STEPS - 1:
            last = turn == STEPS - 2
            bottom, message, cols, head, tail = call(
                functools.partial(after_kernel, last),
                (
                    shape(nx, ny), shape(n_flow, 8 + SLOTS if last else 8, LANES),
                    shape(nx, ny), shape(nz, ny), shape(nz, ny),
                ),
                17,
            )(got, base, cols, head, tail, inlet, *scan, hit, hitcap, reply, weight_t, hit_t)
        else:
            bottom, coolant = call(
                final_kernel, (shape(nx, ny), shape(segs, LANES)), 14, smem=(0,)
            )(me1, got, base, inlet, *scan, hitcap, reply, place, cond)
    solid = solid.at[0].set(bottom)
    return solid, coolant.reshape(channels, stations)


def solution(mesh):
    placed = (
        P(None, "flow", "span"),
        P(None, "flow", "span"),
        P("span", "flow"),
        P("span"),
        P("span"),
        P(("flow", "span"), None),
        P(("flow", "span"), None),
    )
    return jax.shard_map(
        body,
        mesh=mesh,
        in_specs=placed,
        out_specs=(P(None, "flow", "span"), P("span", "flow")),
        check_vma=False,
    )
```

```python
import functools

import jax
import jax.numpy as jnp
from jax import lax
from jax.experimental import pallas as pl
from jax.experimental.pallas import tpu as pltpu
from jax.sharding import PartitionSpec as P

STEPS = 10
KAPPA = 0.16
F32 = jnp.float32
BF16 = jnp.bfloat16
I32 = jnp.int32
HI = lax.Precision.HIGHEST
LANES = 128
SLOTS = 16
TILE = 8
VMEM_LIMIT = 56 << 20


def iota(dims, dim):
    return lax.broadcasted_iota(I32, dims, dim)


def dot(a, b):
    return jnp.dot(a, b, precision=HI, preferred_element_type=F32)


def mul(a, b):
    return jnp.dot(a, b, preferred_element_type=F32)


def parts(x, count):
    found = []
    for _ in range(count):
        found.append(x.astype(BF16))
        x = x - found[-1].astype(F32)
    return found


def dot_t(a, b):
    return lax.dot_general(
        a, b, (((1,), (1,)), ((), ())), precision=HI, preferred_element_type=F32
    )


def pick(values, index):
    return jnp.take_along_axis(values, index, axis=1, mode="promise_in_bounds")


def spec(dims, dtype=F32):
    return jax.ShapeDtypeStruct(dims, dtype)


class Copies:
    def __init__(self, sems):
        self.sems, self.used = sems, 0

    def start(self, source, target):
        copy = pltpu.make_async_copy(source, target, self.sems.at[self.used])
        self.used += 1
        copy.start()
        return copy


def call(kernel, ins, outs, scratch, copies, flops=0, nbytes=0, aliases=None):
    return pl.pallas_call(
        kernel,
        out_shape=outs,
        in_specs=[pl.BlockSpec(memory_space=pl.ANY) for _ in ins],
        out_specs=[pl.BlockSpec(memory_space=pl.ANY) for _ in outs],
        scratch_shapes=[pltpu.VMEM(s.shape, s.dtype) for s in scratch]
        + [pltpu.SemaphoreType.DMA((copies,))],
        compiler_params=pltpu.CompilerParams(vmem_limit_bytes=VMEM_LIMIT),
        cost_estimate=pl.CostEstimate(flops=flops, bytes_accessed=nbytes, transcendentals=0),
        input_output_aliases=aliases or {},
    )(*ins)


def load_segments(copies, cond_hbm, cond):
    return [
        copies.start(cond_hbm.at[:, pl.ds(s * LANES, LANES)], cond.at[:, s, :])
        for s in range(cond.shape[1])
    ]


def source_kernel(
    owner_hbm, row_hbm, cond_hbm, pay_hbm, place_hbm, owner, row, cond, pay, place, sems
):
    copies = Copies(sems)
    first = [copies.start(owner_hbm, owner), copies.start(row_hbm, row)]
    later = load_segments(copies, cond_hbm, cond)
    for copy in first:
        copy.wait()
    segs = owner.shape[0] * LANES
    n_flow = pay.shape[0]
    slots = n_flow * SLOTS
    sub, lane = iota((segs, segs), 0), iota((segs, segs), 1)
    own_row = jnp.concatenate([owner[0:1, :], owner[1:2, :]], axis=1)
    wall_row = jnp.concatenate([row[0:1, :], row[1:2, :]], axis=1)

    def column(line):
        return jnp.sum(jnp.where(sub == lane, line, 0).astype(F32), axis=1, keepdims=True)

    own_col = column(own_row).astype(I32)
    same = own_col == own_row
    rank_row = jnp.sum((same & (sub < lane)).astype(F32), axis=0, keepdims=True).astype(I32)
    rank_col = jnp.sum((same & (lane < sub)).astype(F32), axis=1, keepdims=True).astype(I32)
    slot_row = own_row * SLOTS + rank_row
    slot_col = own_col * SLOTS + rank_col
    place[...] = (iota((segs, slots), 1) == slot_col).astype(F32).astype(BF16)
    out = copies.start(place, place_hbm)
    lanes = iota((segs, LANES), 1)
    value = jnp.where(lanes < SLOTS, column(wall_row).astype(I32), iota((segs, LANES), 0))
    value = jnp.where((lanes < 2 * SLOTS) & (lanes % SLOTS == rank_col), value, 0)
    held = (iota((n_flow, segs), 0) == own_row).astype(F32)
    meta = mul(held.astype(BF16), value.astype(F32).astype(BF16))
    for copy in later:
        copy.wait()
    cond_rows = cond[...].reshape(segs, LANES)
    chosen = (iota((slots, segs), 0) == slot_row).astype(F32).astype(BF16)
    moved = sum(mul(chosen, part) for part in parts(cond_rows, 3))
    total = dot_t(jnp.ones((TILE, LANES), F32), cond_rows)[0:1]
    sub8 = iota((TILE, LANES), 0)
    common = jnp.zeros((TILE, LANES), F32)
    slot_f = slot_row.astype(F32)
    for half in range(2):
        cols = slice(half * LANES, (half + 1) * LANES)
        common = jnp.where(sub8 == 1 + half, slot_f[:, cols], common)
        common = jnp.where(sub8 == 3 + half, total[:, cols], common)
    for p in range(n_flow):
        pay[p, 0:SLOTS, :] = moved[p * SLOTS : (p + 1) * SLOTS]
        pay[p, SLOTS : SLOTS + TILE, :] = jnp.where(sub8 == 0, meta[p : p + 1], common)
    back = copies.start(pay, pay_hbm)
    out.wait()
    back.wait()


def outer_kernel(solid_hbm, bottom_hbm, cols_hbm, head_hbm, tail_hbm, solid, cols, head, tail, sems):
    copies = Copies(sems)
    copies.start(solid_hbm, solid).wait()
    nz, nx, ny = solid.shape
    back = [copies.start(solid.at[0], bottom_hbm)]
    lane = iota((nx, ny), 1)
    ends = jnp.where(lane < nz, 0, ny - 1)
    unroll = 4

    def some(i, found):
        for j in range(unroll):
            z = i * unroll + j
            layer = solid[z]
            head[pl.ds(z, 1), :] = layer[0:1]
            tail[pl.ds(z, 1), :] = layer[nx - 1 : nx]
            found = jnp.where(lane % nz == z, pick(layer, ends), found)
        return found

    found = lax.fori_loop(0, nz // unroll, some, jnp.zeros((nx, ny), F32))
    cols[...] = found
    head[0:1, :] = jnp.zeros((1, ny), F32)
    tail[0:1, :] = jnp.zeros((1, ny), F32)
    for source, target in ((cols, cols_hbm), (head, head_hbm), (tail, tail_hbm)):
        back.append(copies.start(source, target))
    for copy in back:
        copy.wait()


def owner_kernel(
    got_hbm, bottom_hbm, const_hbm,
    hit_hbm, hit_t_hbm, reply_hbm, weight_hbm, swell_hbm,
    index_hbm, scan_hbm, msg_hbm,
    got, bottom, const, hit, hit_t, reply, weight, swell, index, scan, msg, sems,
):
    copies = Copies(sems)
    for copy in [
        copies.start(got_hbm, got), copies.start(bottom_hbm, bottom), copies.start(const_hbm, const)
    ]:
        copy.wait()
    n_flow = got.shape[0]
    slots = n_flow * SLOTS
    block_rows = bottom.shape[0]
    meta = got[:, SLOTS, :]
    lane8, sub8 = iota((TILE, LANES), 1), iota((TILE, LANES), 0)
    mine = lane8 // SLOTS == sub8
    hits, caps = [], []
    n_grp = n_flow // TILE
    rows = iota((LANES, LANES), 0)
    cap8 = jnp.broadcast_to(const[0:1, :], (TILE, LANES))
    for g in range(n_grp):
        part = meta[g * TILE : (g + 1) * TILE]
        row = jnp.sum(jnp.where(mine, pick(part, lane8 % SLOTS), 0.0), axis=0, keepdims=True)
        seg = jnp.where(mine, pick(part, SLOTS + lane8 % SLOTS), 0.0)
        seg = jnp.sum(seg, axis=0, keepdims=True).astype(I32)
        seg8 = jnp.broadcast_to(seg, (TILE, LANES))
        index[4, g * TILE : (g + 1) * TILE, :] = seg8
        cap = pick(cap8, seg8 // 16)[0:1]
        hits.append((rows == row.astype(I32)).astype(F32))
        caps.append(jnp.transpose(jnp.broadcast_to(cap, (LANES, LANES))))
    all_hit = jnp.concatenate(hits, axis=1)
    own_hit = all_hit[0:block_rows]
    hit[...] = own_hit.astype(BF16)
    cond = got[:, 0:SLOTS, :].reshape(slots, LANES)
    sub_t, lane_t = iota((LANES, LANES), 0), iota((LANES, LANES), 1)
    after = sum(
        mul(part, (sub_t > lane_t).astype(F32).astype(BF16)) for part in parts(cond, 3)
    )
    decay = jnp.exp(-cond)
    own_rate = 1.0 - decay
    halves = parts(jnp.transpose(own_rate * jnp.exp(-after)), 2)
    for half in range(2):
        weight[half] = halves[half]
    write_message(bottom[...], weight, own_hit, msg)
    back = [copies.start(msg, msg_hbm), copies.start(weight, weight_hbm)]
    back.append(copies.start(hit, hit_hbm))
    hit_t[...] = jnp.transpose(all_hit).astype(BF16)
    back.append(copies.start(hit_t, hit_t_hbm))
    own_caprate = own_rate * jnp.concatenate(caps, axis=0)
    ahead = sum(
        mul(part, (sub_t < lane_t).astype(F32).astype(BF16)) for part in parts(cond, 3)
    )
    halves = parts(own_caprate * jnp.exp(-ahead), 2)
    for half in range(2):
        reply[half] = halves[half]
    back.append(copies.start(reply, reply_hbm))
    middle = jnp.sum(
        jnp.where(iota((slots, LANES), 1) < LANES // 2, cond, 0.0), axis=1, keepdims=True
    )
    swell[0] = own_rate * jnp.exp(ahead + cond - middle)
    swell[1] = jnp.exp(middle - ahead)
    swell[2] = own_caprate
    back.append(copies.start(swell, swell_hbm))
    lane_f, sub_f = iota((n_flow, LANES), 1), iota((n_flow, LANES), 0)
    inlet = jnp.broadcast_to(const[1:2, :], (n_flow, LANES))
    for half in range(2):
        slot = got[:, SLOTS + 1 + half, :].astype(I32)
        index[half] = (sub_f % TILE) * SLOTS + slot % SLOTS
        index[2 + half] = slot // SLOTS
        gain = jnp.exp(-got[:, SLOTS + 3 + half, :])
        inner = lane_f % 16
        for step in range(4):
            width = 1 << step
            scan[step, half] = jnp.where(inner >= width, gain, 0.0)
            gain = gain * jnp.where(inner >= width, pltpu.roll(gain, width, 1), 1.0)
        scan[10, half] = jnp.where(inner == 0, 1.0, pltpu.roll(gain, 1, 1))
        scan[9, half] = gain
        for step in range(5):
            width = 1 << step
            scan[4 + step, half] = jnp.where(sub_f >= width, gain, 0.0)
            gain = gain * jnp.where(sub_f >= width, pltpu.roll(gain, width, 0), 1.0)
        scan[11, half] = pick(inlet, lane_f // 16 + 8 * half)
    back += [copies.start(index, index_hbm), copies.start(scan, scan_hbm)]
    for copy in back:
        copy.wait()


def write_message(bottom, weight, hit, msg):
    high, low = parts(bottom, 2)
    ends = mul(high, weight[0]) + (mul(high, weight[1]) + mul(low, weight[0]))
    ends = jnp.sum(ends * hit, axis=0, keepdims=True)
    sub8 = iota((TILE, LANES), 0)
    tile = jnp.where(sub8 == 4, bottom[0:1], bottom[bottom.shape[0] - 1 :])
    for g in range(ends.shape[1] // LANES):
        tile = jnp.where(sub8 == g, ends[:, g * LANES : (g + 1) * LANES], tile)
    for p in range(msg.shape[0]):
        msg[p, 0:TILE, :] = tile


def march_kernel(
    bottom_hbm, hit_hbm, hit_t_hbm, swell_hbm, sink_hbm,
    bottom, hit, hit_t, swell, sink, flux, sems,
):
    copies = Copies(sems)
    first = [copies.start(bottom_hbm, bottom), copies.start(hit_t_hbm, hit_t)]
    slots = hit_t.shape[0]
    piece = slots // 4
    then = []
    for i in range(4):
        rows = pl.ds(i * piece, piece)
        then.append(copies.start(swell_hbm.at[:, rows, :], swell.at[:, rows, :]))
    last = copies.start(hit_hbm, hit)
    for copy in first:
        copy.wait()
    nx, ny = bottom.shape
    padded = jnp.concatenate([bottom[...], jnp.zeros((LANES - nx, ny), F32)], axis=0)
    wide = jnp.concatenate(parts(padded, 3), axis=1)
    earlier = (iota((LANES, LANES), 0) < iota((LANES, LANES), 1)).astype(F32).astype(BF16)
    for i in range(4):
        then[i].wait()
        rows = pl.ds(i * piece, piece)
        triple = mul(hit_t[rows, :], wide)
        temp = (triple[:, 0:ny] + triple[:, ny : 2 * ny]) + triple[:, 2 * ny :]
        high, low = parts(swell[0, rows, :] * temp, 2)
        before = swell[1, rows, :] * (mul(high, earlier) + mul(low, earlier))
        high, low = parts(swell[2, rows, :] * (temp - before), 2)
        flux[0, rows, :] = high
        flux[1, rows, :] = low
    last.wait()
    sink[...] = mul(hit[...], flux[0]) + mul(hit[...], flux[1])
    copies.start(sink, sink_hbm).wait()


def conduct_kernel(
    solid_hbm, bottom_hbm, heat_hbm, west_hbm, east_hbm, north_hbm, south_hbm, sink_hbm,
    out_hbm, base_hbm, cols_hbm, head_hbm, tail_hbm,
    solid, heat, west, east, sink, out, base, cols, head, tail, sems,
):
    nz, nx, ny = out.shape
    copies = Copies(sems)
    inner = pl.ds(8, nx)
    early = [
        copies.start(bottom_hbm, solid.at[1, inner, :]),
        copies.start(north_hbm, solid.at[pl.ds(1, nz), 7, :]),
        copies.start(south_hbm, solid.at[pl.ds(1, nz), 8 + nx, :]),
        copies.start(west_hbm, west),
        copies.start(east_hbm, east),
        copies.start(sink_hbm, sink),
    ]
    pieces = 4
    chunk = nz // pieces
    solids, heats = [], []
    for p in range(pieces):
        count = chunk if p < pieces - 1 else chunk - 1
        source = solid_hbm.at[pl.ds(p * chunk + 1, count)]
        solids.append(copies.start(source, solid.at[pl.ds(p * chunk + 2, count), inner, :]))
        piece = pl.ds(p * chunk, chunk)
        heats.append(copies.start(heat_hbm.at[piece], heat.at[piece]))
    me, lot = lax.axis_index("flow"), lax.axis_index("span")
    n_flow, n_span = lax.axis_size("flow"), lax.axis_size("span")
    lane = iota((nx, ny), 1)
    border = (lane == 0) | (lane == ny - 1)
    ends = jnp.where(lane < nz, 0, ny - 1)
    solid[0, inner, :] = jnp.zeros((nx, ny), F32)
    solid[nz + 1, inner, :] = jnp.zeros((nx, ny), F32)
    for copy in early:
        copy.wait()

    @pl.when(me == 0)
    def _():
        solid[pl.ds(1, nz), 7, :] = jnp.zeros((nz, ny), F32)

    @pl.when(me == n_flow - 1)
    def _():
        solid[pl.ds(1, nz), 8 + nx, :] = jnp.zeros((nz, ny), F32)

    halo = jnp.where((lane < nz) & (lot < n_span - 1), east[...], 0.0)
    halo = jnp.where((lane >= nz) & (lot > 0), west[...], halo)
    unroll = 4

    def some(start, i, found):
        for j in range(unroll):
            z = start + i * unroll + j
            mid = solid[z + 1, inner, :]
            side = pick(halo, jnp.where(lane == 0, nz, 0) + z)
            right, left = pltpu.roll(mid, 1, 1), pltpu.roll(mid, ny - 1, 1)
            across = jnp.where(border, side + jnp.where(lane == 0, left, right), left + right)
            total = across + (solid[z + 1, pl.ds(7, nx), :] + solid[z + 1, pl.ds(9, nx), :])
            total = total + (solid[z, inner, :] + solid[z + 2, inner, :])
            new = mid + KAPPA * (total - 6.0 * mid) + heat[z]
            out[z] = new
            head[pl.ds(z, 1), :] = new[0:1]
            tail[pl.ds(z, 1), :] = new[nx - 1 : nx]
            found = jnp.where(lane % nz == z, pick(new, ends), found)
        return found

    found = jnp.zeros((nx, ny), F32)
    back = []
    for p in range(pieces):
        solids[p].wait()
        heats[p].wait()
        found = lax.fori_loop(0, chunk // unroll, functools.partial(some, p * chunk), found)
        piece = pl.ds(p * chunk, chunk)
        back.append(copies.start(out.at[piece], out_hbm.at[piece]))
    cols[...] = found
    head[0:1, :] = jnp.zeros((1, ny), F32)
    tail[0:1, :] = jnp.zeros((1, ny), F32)
    base[...] = out[0] - sink[...]
    for source, target in (
        (cols, cols_hbm), (head, head_hbm), (tail, tail_hbm), (base, base_hbm)
    ):
        back.append(copies.start(source, target))
    for copy in back:
        copy.wait()


def entering(got, index, scan):
    n_flow = got.shape[0]
    ends = [[], []]
    for g in range(n_flow // TILE):
        rows = slice(g * TILE, (g + 1) * TILE)
        lanes = [index[half, rows, :] for half in range(2)]
        origin = [index[2 + half, rows, :] for half in range(2)]
        acc = [jnp.zeros((TILE, LANES), F32) for _ in range(2)]
        for o in range(n_flow):
            line = jnp.broadcast_to(got[o, g : g + 1, :], (TILE, LANES))
            for half in range(2):
                acc[half] = jnp.where(origin[half] == o, pick(line, lanes[half]), acc[half])
        for half in range(2):
            ends[half].append(acc[half])
    result = []
    sub, lane = iota((n_flow, LANES), 0), iota((n_flow, LANES), 1)
    for half in range(2):
        x = jnp.concatenate(ends[half], axis=0)
        for step in range(4):
            x = x + scan[step, half] * pltpu.roll(x, 1 << step, 1)
        inlet = scan[11, half]
        y = jnp.where(sub == 0, x + scan[9, half] * inlet, x)
        for step in range(5):
            y = y + scan[4 + step, half] * pltpu.roll(y, 1 << step, 0)
        carry = jnp.where(sub == 0, inlet, pltpu.roll(y, 1, 0))
        carry = pick(carry, lane // 16 * 16 + 15)
        earlier = jnp.where(lane % 16 == 0, 0.0, pltpu.roll(x, 1, 1))
        result.append(earlier + scan[10, half] * carry)
    return result


def hosted(enter, index):
    lane8, sub8 = iota((TILE, LANES), 1), iota((TILE, LANES), 0)
    found = []
    for g in range(enter[0].shape[0] // TILE):
        rows = slice(g * TILE, (g + 1) * TILE)
        seg = index[4, rows, :]
        low, high = (pick(enter[half][rows], seg % LANES) for half in range(2))
        value = jnp.where(lane8 // SLOTS == sub8, jnp.where(seg < LANES, low, high), 0.0)
        found.append(jnp.sum(value, axis=0, keepdims=True))
    return jnp.concatenate(found, axis=1)


def new_bottom(got, carry, base, hit, reply):
    me, n_flow = lax.axis_index("flow"), got.shape[0]
    nx, ny = base.shape
    high, low = parts(carry, 2)
    high, low = hit * high, hit * low
    bottom = base[...] + (mul(high, reply[0]) + (mul(high, reply[1]) + mul(low, reply[0])))
    north = got[jnp.maximum(me - 1, 0), 5:6, :]
    south = got[jnp.minimum(me + 1, n_flow - 1), 4:5, :]
    sub = iota((nx, ny), 0)
    halo = jnp.where((sub == 0) & (me > 0), north, 0.0)
    halo = halo + jnp.where((sub == nx - 1) & (me < n_flow - 1), south, 0.0)
    return bottom + KAPPA * halo


def after_kernel(
    last,
    got_hbm, base_hbm, plain_hbm, index_hbm, scan_hbm, hit_hbm, reply_hbm, weight_hbm,
    hit_t_hbm, bottom_hbm, msg_hbm, cols_hbm,
    got, base, plain, index, scan, hit, reply, weight, hit_t, bottom, msg, cols, sems,
):
    copies = Copies(sems)
    first = [copies.start(got_hbm, got), copies.start(index_hbm, index), copies.start(scan_hbm, scan)]
    then = [
        copies.start(hit_hbm, hit), copies.start(reply_hbm, reply), copies.start(base_hbm, base),
        copies.start(plain_hbm, plain), copies.start(weight_hbm, weight),
    ]
    if last:
        then.append(copies.start(hit_t_hbm, hit_t))
    for copy in first:
        copy.wait()
    carry = hosted(entering(got, index, scan), index)
    for copy in then:
        copy.wait()
    own_hit = hit[...]
    new = new_bottom(got, carry, base, own_hit, reply)
    bottom[...] = new
    back = [copies.start(bottom, bottom_hbm)]
    nx, ny = new.shape
    nz = LANES // 4
    lane = iota((nx, ny), 1)
    cols[...] = jnp.where(
        lane % nz == 0, pick(new, jnp.where(lane < nz, 0, ny - 1)), plain[...]
    )
    back.append(copies.start(cols, cols_hbm))
    if last:
        padded = jnp.concatenate([new, jnp.zeros((LANES - nx, ny), F32)], axis=0)
        temp = sum(mul(hit_t[...], part) for part in parts(padded, 3))
        for p in range(msg.shape[0]):
            msg[p, TILE : TILE + SLOTS, :] = temp[p * SLOTS : (p + 1) * SLOTS]
    write_message(new, weight, own_hit.astype(F32), msg)
    back.append(copies.start(msg, msg_hbm))
    for copy in back:
        copy.wait()


def final_kernel(
    got_hbm, base_hbm, index_hbm, scan_hbm, hit_hbm, reply_hbm,
    place_hbm, cond_hbm, solid_hbm, out_hbm, coolant_hbm,
    got, base, index, scan, hit, reply, place, cond, bottom, coolant, sems,
):
    del solid_hbm
    copies = Copies(sems)
    first = [copies.start(got_hbm, got), copies.start(index_hbm, index), copies.start(scan_hbm, scan)]
    then = [
        copies.start(hit_hbm, hit), copies.start(reply_hbm, reply), copies.start(base_hbm, base),
        copies.start(place_hbm, place),
    ]
    then += load_segments(copies, cond_hbm, cond)
    for copy in first:
        copy.wait()
    enter = entering(got, index, scan)
    carry = hosted(enter, index)
    for copy in then:
        copy.wait()
    bottom[...] = new_bottom(got, carry, base, hit[...], reply)
    back = [copies.start(bottom, out_hbm.at[0])]
    n_flow = got.shape[0]
    temps = got[:, TILE : TILE + SLOTS, :].reshape(n_flow * SLOTS, LANES)
    temp = sum(mul(place[...], part) for part in parts(temps, 3))
    segs = temp.shape[0]
    lane = iota((segs, LANES), 1)
    gain = jnp.exp(-cond[...].reshape(segs, LANES))
    shift = (1.0 - gain) * temp
    for step in range(7):
        width = 1 << step
        shift = shift + jnp.where(lane >= width, gain * pltpu.roll(shift, width, 1), 0.0)
        gain = gain * jnp.where(lane >= width, pltpu.roll(gain, width, 1), 1.0)
    own = iota((n_flow, LANES), 0) == lax.axis_index("flow")
    line = jnp.concatenate(
        [jnp.sum(jnp.where(own, part, 0.0), axis=0, keepdims=True) for part in enter], axis=1
    )
    same = iota((segs, segs), 0) == iota((segs, segs), 1)
    start = jnp.sum(jnp.where(same, line, 0.0), axis=1, keepdims=True)
    coolant[...] = (shift + gain * start).reshape(coolant.shape)
    for s in range(coolant.shape[1]):
        target = coolant_hbm.at[:, pl.ds(s * LANES, LANES)]
        back.append(copies.start(coolant.at[:, s, :], target))
    for copy in back:
        copy.wait()


def body(solid_start, heat_gen, conductance, heat_capacity, inlet_temp, wall_owner, wall_row):
    n_flow, n_span = lax.axis_size("flow"), lax.axis_size("span")
    nz, nx, ny = solid_start.shape
    channels, stations = conductance.shape
    segs = wall_owner.shape[0]
    slots = n_flow * SLOTS
    const = jnp.pad(
        jnp.stack([heat_capacity, inlet_temp]), ((0, TILE - 2), (0, LANES - channels))
    )

    def both_ways(ahead, back, axis, size):
        up = [(i, (i + 1) % size) for i in range(size)]
        down = [(i, (i - 1) % size) for i in range(size)]
        return lax.ppermute(ahead, axis, up), lax.ppermute(back, axis, down)

    def exchange(message):
        return lax.all_to_all(message, "flow", 0, 0, tiled=True)

    lines = spec((segs // LANES, LANES), I32)
    split = spec((channels, segs // channels, LANES))
    layer, edge = spec((nx, ny)), spec((nz, ny))
    block = spec((nz, nx, ny))
    pay_spec, place_spec = spec((n_flow, SLOTS + TILE, LANES)), spec((segs, slots), BF16)
    pay, place = call(
        source_kernel,
        (wall_owner.reshape(lines.shape), wall_row.reshape(lines.shape), conductance),
        (pay_spec, place_spec),
        (lines, lines, split, pay_spec, place_spec),
        20,
    )
    got = exchange(pay)
    bottom, cols, head, tail = call(
        outer_kernel, (solid_start,), (layer, layer, edge, edge), (block, layer, edge, edge), 5
    )
    hit_spec, hit_t_spec = spec((nx, slots), BF16), spec((slots, LANES), BF16)
    reply_spec, weight_spec = spec((2, slots, LANES), BF16), spec((2, LANES, slots), BF16)
    swell_spec = spec((3, slots, LANES))
    index_spec, scan_spec = spec((5, n_flow, LANES), I32), spec((12, 2, n_flow, LANES))
    msg_spec, long_spec = spec((n_flow, TILE, LANES)), spec((n_flow, TILE + SLOTS, LANES))
    constants = (
        hit_spec, hit_t_spec, reply_spec, weight_spec, swell_spec, index_spec, scan_spec, msg_spec,
    )
    hit, hit_t, reply, weight, swell, index, scan, message = call(
        owner_kernel,
        (got, bottom, const),
        constants,
        (pay_spec, layer, spec((TILE, LANES)), *constants),
        11,
    )

    def beside(solid, bottom, cols, north, south, message):
        got = exchange(message)
        west, east = both_ways(cols, cols, "span", n_span)
        (sink,) = call(
            march_kernel,
            (bottom, hit, hit_t, swell),
            (layer,),
            (layer, hit_spec, hit_t_spec, swell_spec, layer, reply_spec),
            8,
            flops=2_000_000,
            nbytes=3_000_000,
        )
        solid, base, cols, head, tail = call(
            conduct_kernel,
            (solid, bottom, heat_gen, west, east, north, south, sink),
            (block, layer, layer, edge, edge),
            (
                spec((nz + 2, nx + 16, ny)), block, layer, layer, layer,
                block, layer, layer, edge, edge,
            ),
            22,
            flops=4_000_000,
            nbytes=6_000_000,
            aliases={0: 0},
        )
        return got, solid, base, cols, head, tail

    def step(state, last=False):
        got, solid, base, cols, head, tail = beside(*state)
        north, south = both_ways(tail, head, "flow", n_flow)
        sent = long_spec if last else msg_spec
        bottom, message, cols = call(
            functools.partial(after_kernel, last),
            (got, base, cols, index, scan, hit, reply, weight, hit_t),
            (layer, sent, layer),
            (
                msg_spec, layer, layer, index_spec, scan_spec, hit_spec, reply_spec, weight_spec,
                hit_t_spec, layer, sent, layer,
            ),
            13,
            flops=4_000_000,
            nbytes=4_000_000,
        )
        return solid, bottom, cols, north, south, message

    north, south = both_ways(tail, head, "flow", n_flow)
    state = (solid_start, bottom, cols, north, south, message)
    state = lax.fori_loop(0, STEPS - 2, lambda turn, now: step(now), state)
    state = step(state, last=True)
    got, solid, base, _, _, _ = beside(*state)
    return call(
        final_kernel,
        (got, base, index, scan, hit, reply, place, conductance, solid),
        (block, spec((channels, stations))),
        (
            long_spec, layer, index_spec, scan_spec, hit_spec, reply_spec, place_spec, split,
            layer, split,
        ),
        8 + 2 * split.shape[1],
        aliases={8: 0},
    )


def solution(mesh):
    placed = (
        P(None, "flow", "span"),
        P(None, "flow", "span"),
        P("span", "flow"),
        P("span"),
        P("span"),
        P(("flow", "span"), None),
        P(("flow", "span"), None),
    )
    return jax.shard_map(
        body,
        mesh=mesh,
        in_specs=placed,
        out_specs=(P(None, "flow", "span"), P("span", "flow")),
        check_vma=False,
    )
```

```python
import functools

import jax
import jax.numpy as jnp
from jax import lax
from jax.experimental import pallas as pl
from jax.experimental.pallas import tpu as pltpu
from jax.sharding import PartitionSpec as P

STEPS = 10
KAPPA = 0.16
F32 = jnp.float32
BF16 = jnp.bfloat16
I32 = jnp.int32
HI = lax.Precision.HIGHEST
LANES = 128
SLOTS = 16
TILE = 8
VMEM_LIMIT = 16 << 20


def iota(dims, dim):
    return lax.broadcasted_iota(I32, dims, dim)


def dot(a, b):
    return jnp.dot(a, b, precision=HI, preferred_element_type=F32)


def mul(a, b):
    return jnp.dot(a, b, preferred_element_type=F32)


def parts(x, count):
    found = []
    for _ in range(count):
        found.append(x.astype(BF16))
        x = x - found[-1].astype(F32)
    return found


def dot_t(a, b):
    return lax.dot_general(
        a, b, (((1,), (1,)), ((), ())), precision=HI, preferred_element_type=F32
    )


def pick(values, index):
    return jnp.take_along_axis(values, index, axis=1, mode="promise_in_bounds")


def spec(dims, dtype=F32):
    return jax.ShapeDtypeStruct(dims, dtype)


class Copies:
    def __init__(self, sems):
        self.sems, self.used = sems, 0

    def start(self, source, target):
        copy = pltpu.make_async_copy(source, target, self.sems.at[self.used])
        self.used += 1
        copy.start()
        return copy


def call(kernel, ins, outs, scratch, copies, held=(), held_out=(), flops=0, nbytes=0, aliases=None):
    return pl.pallas_call(
        kernel,
        out_shape=outs,
        in_specs=[
            pl.BlockSpec(memory_space=pltpu.VMEM if k in held else pltpu.HBM)
            for k in range(len(ins))
        ],
        out_specs=[
            pl.BlockSpec(memory_space=pltpu.VMEM if k in held_out else pltpu.HBM)
            for k in range(len(outs))
        ],
        scratch_shapes=[pltpu.VMEM(s.shape, s.dtype) for s in scratch]
        + [pltpu.SemaphoreType.DMA((copies,))],
        compiler_params=pltpu.CompilerParams(vmem_limit_bytes=VMEM_LIMIT),
        cost_estimate=pl.CostEstimate(flops=flops, bytes_accessed=nbytes, transcendentals=0),
        input_output_aliases=aliases or {},
    )(*ins)


def load_segments(copies, cond_hbm, cond):
    return [
        copies.start(cond_hbm.at[:, pl.ds(s * LANES, LANES)], cond.at[:, s, :])
        for s in range(cond.shape[1])
    ]


def source_kernel(
    owner_hbm, row_hbm, cond_hbm, pay_hbm, place_hbm, owner, row, cond, pay, place, sems
):
    copies = Copies(sems)
    first = [copies.start(owner_hbm, owner), copies.start(row_hbm, row)]
    later = load_segments(copies, cond_hbm, cond)
    for copy in first:
        copy.wait()
    segs = owner.shape[0] * LANES
    n_flow = pay.shape[0]
    slots = n_flow * SLOTS
    sub, lane = iota((segs, segs), 0), iota((segs, segs), 1)
    own_row = jnp.concatenate([owner[0:1, :], owner[1:2, :]], axis=1)
    wall_row = jnp.concatenate([row[0:1, :], row[1:2, :]], axis=1)

    def column(line):
        return jnp.sum(jnp.where(sub == lane, line, 0).astype(F32), axis=1, keepdims=True)

    own_col = column(own_row).astype(I32)
    same = own_col == own_row
    rank_row = jnp.sum((same & (sub < lane)).astype(F32), axis=0, keepdims=True).astype(I32)
    rank_col = jnp.sum((same & (lane < sub)).astype(F32), axis=1, keepdims=True).astype(I32)
    slot_row = own_row * SLOTS + rank_row
    slot_col = own_col * SLOTS + rank_col
    place[...] = (iota((segs, slots), 1) == slot_col).astype(F32).astype(BF16)
    out = copies.start(place, place_hbm)
    lanes = iota((segs, LANES), 1)
    value = jnp.where(lanes < SLOTS, column(wall_row).astype(I32), iota((segs, LANES), 0))
    value = jnp.where((lanes < 2 * SLOTS) & (lanes % SLOTS == rank_col), value, 0)
    held = (iota((n_flow, segs), 0) == own_row).astype(F32)
    meta = mul(held.astype(BF16), value.astype(F32).astype(BF16))
    for copy in later:
        copy.wait()
    cond_rows = cond[...].reshape(segs, LANES)
    chosen = (iota((slots, segs), 0) == slot_row).astype(F32).astype(BF16)
    moved = sum(mul(chosen, part) for part in parts(cond_rows, 3))
    total = dot_t(jnp.ones((TILE, LANES), F32), cond_rows)[0:1]
    sub8 = iota((TILE, LANES), 0)
    common = jnp.zeros((TILE, LANES), F32)
    slot_f = slot_row.astype(F32)
    for half in range(2):
        cols = slice(half * LANES, (half + 1) * LANES)
        common = jnp.where(sub8 == 1 + half, slot_f[:, cols], common)
        common = jnp.where(sub8 == 3 + half, total[:, cols], common)
    for p in range(n_flow):
        pay[p, 0:SLOTS, :] = moved[p * SLOTS : (p + 1) * SLOTS]
        pay[p, SLOTS : SLOTS + TILE, :] = jnp.where(sub8 == 0, meta[p : p + 1], common)
    back = copies.start(pay, pay_hbm)
    out.wait()
    back.wait()


def outer_kernel(solid_hbm, heat_hbm, solid, heat, cols_hbm, cols, sems):
    copies = Copies(sems)
    nz, nx, ny = heat.shape
    inner = pl.ds(8, nx)
    warm = copies.start(heat_hbm, heat)
    copies.start(solid_hbm, solid.at[pl.ds(1, nz), inner, :]).wait()
    lane = iota((nx, ny), 1)
    ends = jnp.where(lane < nz, 0, ny - 1)
    solid[0, inner, :] = jnp.zeros((nx, ny), F32)
    solid[nz + 1, inner, :] = jnp.zeros((nx, ny), F32)
    solid[pl.ds(1, nz), 7, :] = jnp.zeros((nz, ny), F32)
    solid[pl.ds(1, nz), 8 + nx, :] = jnp.zeros((nz, ny), F32)
    unroll = 4

    def some(i, found):
        for j in range(unroll):
            z = i * unroll + j
            found = jnp.where(lane % nz == z, pick(solid[z + 1, inner, :], ends), found)
        return found

    cols[...] = lax.fori_loop(0, nz // unroll, some, jnp.zeros((nx, ny), F32))
    back = copies.start(cols, cols_hbm)
    warm.wait()
    back.wait()


def owner_kernel(
    got_hbm, solid, const_hbm,
    hit, hit_t, reply, weight, swell, index, scan, msg_hbm,
    got, const, msg, edges, sems,
):
    copies = Copies(sems)
    for copy in [copies.start(got_hbm, got), copies.start(const_hbm, const)]:
        copy.wait()
    bottom = solid[1, pl.ds(8, hit.shape[0]), :]
    n_flow = got.shape[0]
    slots = n_flow * SLOTS
    block_rows = bottom.shape[0]
    meta = got[:, SLOTS, :]
    lane8, sub8 = iota((TILE, LANES), 1), iota((TILE, LANES), 0)
    mine = lane8 // SLOTS == sub8
    hits, caps = [], []
    n_grp = n_flow // TILE
    rows = iota((LANES, LANES), 0)
    cap8 = jnp.broadcast_to(const[0:1, :], (TILE, LANES))
    for g in range(n_grp):
        part = meta[g * TILE : (g + 1) * TILE]
        row = jnp.sum(jnp.where(mine, pick(part, lane8 % SLOTS), 0.0), axis=0, keepdims=True)
        seg = jnp.where(mine, pick(part, SLOTS + lane8 % SLOTS), 0.0)
        seg = jnp.sum(seg, axis=0, keepdims=True).astype(I32)
        seg8 = jnp.broadcast_to(seg, (TILE, LANES))
        index[4, g * TILE : (g + 1) * TILE, :] = seg8
        cap = pick(cap8, seg8 // 16)[0:1]
        hits.append((rows == row.astype(I32)).astype(F32))
        caps.append(jnp.transpose(jnp.broadcast_to(cap, (LANES, LANES))))
    all_hit = jnp.concatenate(hits, axis=1)
    own_hit = all_hit[0:block_rows]
    hit[...] = own_hit.astype(BF16)
    cond = got[:, 0:SLOTS, :].reshape(slots, LANES)
    sub_t, lane_t = iota((LANES, LANES), 0), iota((LANES, LANES), 1)
    after = sum(
        mul(part, (sub_t > lane_t).astype(F32).astype(BF16)) for part in parts(cond, 3)
    )
    decay = jnp.exp(-cond)
    own_rate = 1.0 - decay
    halves = parts(jnp.transpose(own_rate * jnp.exp(-after)), 2)
    for half in range(2):
        weight[half] = halves[half]
    write_shifts(bottom, weight, own_hit, msg)
    back = send_message(copies, solid, msg, edges, msg_hbm)
    hit_t[...] = jnp.transpose(all_hit).astype(BF16)
    own_caprate = own_rate * jnp.concatenate(caps, axis=0)
    ahead = sum(
        mul(part, (sub_t < lane_t).astype(F32).astype(BF16)) for part in parts(cond, 3)
    )
    halves = parts(own_caprate * jnp.exp(-ahead), 2)
    for half in range(2):
        reply[half] = halves[half]
    middle = jnp.sum(
        jnp.where(iota((slots, LANES), 1) < LANES // 2, cond, 0.0), axis=1, keepdims=True
    )
    swell[0] = own_rate * jnp.exp(ahead + cond - middle)
    swell[1] = jnp.exp(middle - ahead)
    swell[2] = own_caprate
    lane_f, sub_f = iota((n_flow, LANES), 1), iota((n_flow, LANES), 0)
    inlet = jnp.broadcast_to(const[1:2, :], (n_flow, LANES))
    for half in range(2):
        slot = got[:, SLOTS + 1 + half, :].astype(I32)
        index[half] = (sub_f % TILE) * SLOTS + slot % SLOTS
        index[2 + half] = slot // SLOTS
        gain = jnp.exp(-got[:, SLOTS + 3 + half, :])
        inner = lane_f % 16
        for step in range(4):
            width = 1 << step
            scan[step, half] = jnp.where(inner >= width, gain, 0.0)
            gain = gain * jnp.where(inner >= width, pltpu.roll(gain, width, 1), 1.0)
        scan[10, half] = jnp.where(inner == 0, 1.0, pltpu.roll(gain, 1, 1))
        scan[9, half] = gain
        for step in range(5):
            width = 1 << step
            scan[4 + step, half] = jnp.where(sub_f >= width, gain, 0.0)
            gain = gain * jnp.where(sub_f >= width, pltpu.roll(gain, width, 0), 1.0)
        scan[11, half] = pick(inlet, lane_f // 16 + 8 * half)
    for copy in back:
        copy.wait()


def write_shifts(bottom, weight, hit, msg):
    high, low = parts(bottom, 2)
    ends = mul(high, weight[0]) + (mul(high, weight[1]) + mul(low, weight[0]))
    ends = jnp.sum(ends * hit, axis=0, keepdims=True)
    sub8 = iota((TILE, LANES), 0)
    tile = jnp.zeros((TILE, LANES), F32)
    for g in range(ends.shape[1] // LANES):
        tile = jnp.where(sub8 == g, ends[:, g * LANES : (g + 1) * LANES], tile)
    for p in range(msg.shape[0]):
        msg[p, 0:TILE, :] = tile


def send_message(copies, solid, msg, edges, msg_hbm):
    n_flow, me = msg.shape[0], lax.axis_index("flow")
    nz, nx = edges.shape[1], solid.shape[1] - 16
    edges[0] = solid[pl.ds(1, nz), 8, :]
    edges[1] = solid[pl.ds(1, nz), 7 + nx, :]
    rows = pl.ds(TILE, nz)
    return [
        copies.start(edges.at[0], msg_hbm.at[lax.rem(me + n_flow - 1, n_flow), rows, :]),
        copies.start(edges.at[1], msg_hbm.at[lax.rem(me + 1, n_flow), rows, :]),
        copies.start(msg.at[:, pl.ds(0, TILE), :], msg_hbm.at[:, pl.ds(0, TILE), :]),
    ]


def take_message(copies, got_hbm, got, edges):
    n_flow, me = got.shape[0], lax.axis_index("flow")
    rows = pl.ds(TILE, edges.shape[1])
    return [
        copies.start(got_hbm.at[:, pl.ds(0, TILE), :], got),
        copies.start(got_hbm.at[lax.rem(me + n_flow - 1, n_flow), rows, :], edges.at[0]),
        copies.start(got_hbm.at[lax.rem(me + 1, n_flow), rows, :], edges.at[1]),
    ]


def add_outer_rows(solid, edges):
    n_flow, me = lax.axis_size("flow"), lax.axis_index("flow")
    nz, nx = edges.shape[1], solid.shape[1] - 16
    north = jnp.where(me > 0, KAPPA * edges[0], 0.0)
    south = jnp.where(me < n_flow - 1, KAPPA * edges[1], 0.0)
    layers = pl.ds(1, nz)
    solid[layers, 8, :] = solid[layers, 8, :] + north
    solid[layers, 7 + nx, :] = solid[layers, 7 + nx, :] + south
    return north, south


def march_kernel(solid, hit, hit_t, swell, sink, flux, sems):
    del sems
    slots = hit_t.shape[0]
    piece = slots // 4
    nx, ny = sink.shape
    bottom = solid[1, pl.ds(8, nx), :]
    padded = jnp.concatenate([bottom, jnp.zeros((LANES - nx, ny), F32)], axis=0)
    wide = jnp.concatenate(parts(padded, 3), axis=1)
    earlier = (iota((LANES, LANES), 0) < iota((LANES, LANES), 1)).astype(F32).astype(BF16)
    for i in range(4):
        rows = pl.ds(i * piece, piece)
        triple = mul(hit_t[rows, :], wide)
        temp = (triple[:, 0:ny] + triple[:, ny : 2 * ny]) + triple[:, 2 * ny :]
        high, low = parts(swell[0, rows, :] * temp, 2)
        before = swell[1, rows, :] * (mul(high, earlier) + mul(low, earlier))
        high, low = parts(swell[2, rows, :] * (temp - before), 2)
        flux[0, rows, :] = high
        flux[1, rows, :] = low
    sink[...] = mul(hit[...], flux[0]) + mul(hit[...], flux[1])


def conduct_kernel(
    old, heat, west_hbm, east_hbm, sink, solid, cols_hbm, west, east, cols, sems
):
    del old
    nz, nx, ny = heat.shape
    copies = Copies(sems)
    inner = pl.ds(8, nx)
    for copy in [
        copies.start(west_hbm, west), copies.start(east_hbm, east)
    ]:
        copy.wait()
    lot, n_span = lax.axis_index("span"), lax.axis_size("span")
    lane = iota((nx, ny), 1)
    border = (lane == 0) | (lane == ny - 1)
    ends = jnp.where(lane < nz, 0, ny - 1)
    halo = jnp.where((lane < nz) & (lot < n_span - 1), east[...], 0.0)
    halo = jnp.where((lane >= nz) & (lot > 0), west[...], halo)
    unroll = 4

    def some(i, state):
        found, low = state
        for j in range(unroll):
            z = i * unroll + j
            mid = solid[z + 1, inner, :]
            side = pick(halo, jnp.where(lane == 0, nz, 0) + z)
            right, left = pltpu.roll(mid, 1, 1), pltpu.roll(mid, ny - 1, 1)
            across = jnp.where(border, side + jnp.where(lane == 0, left, right), left + right)
            total = across + (solid[z + 1, pl.ds(7, nx), :] + solid[z + 1, pl.ds(9, nx), :])
            total = total + (low + solid[z + 2, inner, :])
            new = mid + KAPPA * (total - 6.0 * mid) + heat[z]
            solid[z + 1, inner, :] = new
            found = jnp.where(lane % nz == z, pick(new, ends), found)
            low = mid
        return found, low

    zero = jnp.zeros((nx, ny), F32)
    cols[...], _ = lax.fori_loop(0, nz // unroll, some, (zero, zero))
    back = copies.start(cols, cols_hbm)
    solid[1, inner, :] = solid[1, inner, :] - sink[...]
    back.wait()


def entering(got, index, scan):
    n_flow = got.shape[0]
    ends = [[], []]
    for g in range(n_flow // TILE):
        rows = slice(g * TILE, (g + 1) * TILE)
        lanes = [index[half, rows, :] for half in range(2)]
        origin = [index[2 + half, rows, :] for half in range(2)]
        acc = [jnp.zeros((TILE, LANES), F32) for _ in range(2)]
        for o in range(n_flow):
            line = jnp.broadcast_to(got[o, g : g + 1, :], (TILE, LANES))
            for half in range(2):
                acc[half] = jnp.where(origin[half] == o, pick(line, lanes[half]), acc[half])
        for half in range(2):
            ends[half].append(acc[half])
    result = []
    sub, lane = iota((n_flow, LANES), 0), iota((n_flow, LANES), 1)
    for half in range(2):
        x = jnp.concatenate(ends[half], axis=0)
        for step in range(4):
            x = x + scan[step, half] * pltpu.roll(x, 1 << step, 1)
        inlet = scan[11, half]
        y = jnp.where(sub == 0, x + scan[9, half] * inlet, x)
        for step in range(5):
            y = y + scan[4 + step, half] * pltpu.roll(y, 1 << step, 0)
        carry = jnp.where(sub == 0, inlet, pltpu.roll(y, 1, 0))
        carry = pick(carry, lane // 16 * 16 + 15)
        earlier = jnp.where(lane % 16 == 0, 0.0, pltpu.roll(x, 1, 1))
        result.append(earlier + scan[10, half] * carry)
    return result


def hosted(enter, index):
    lane8, sub8 = iota((TILE, LANES), 1), iota((TILE, LANES), 0)
    found = []
    for g in range(enter[0].shape[0] // TILE):
        rows = slice(g * TILE, (g + 1) * TILE)
        seg = index[4, rows, :]
        low, high = (pick(enter[half][rows], seg % LANES) for half in range(2))
        value = jnp.where(lane8 // SLOTS == sub8, jnp.where(seg < LANES, low, high), 0.0)
        found.append(jnp.sum(value, axis=0, keepdims=True))
    return jnp.concatenate(found, axis=1)


def new_bottom(carry, base, hit, reply):
    high, low = parts(carry, 2)
    high, low = hit * high, hit * low
    return base + (mul(high, reply[0]) + (mul(high, reply[1]) + mul(low, reply[0])))


def after_kernel(
    last,
    got_hbm, old, plain_hbm, index, scan, hit, reply, weight, hit_t,
    solid, msg_hbm, cols_hbm,
    got, edges, plain, msg, cols, sems,
):
    del old
    copies = Copies(sems)
    first, *then = take_message(copies, got_hbm, got, edges)
    then.append(copies.start(plain_hbm, plain))
    first.wait()
    carry = hosted(entering(got, index, scan), index)
    own_hit = hit[...]
    nx = own_hit.shape[0]
    inner = pl.ds(8, nx)
    for copy in then:
        copy.wait()
    north, south = add_outer_rows(solid, edges)
    new = new_bottom(carry, solid[1, inner, :], own_hit, reply)
    solid[1, inner, :] = new
    write_shifts(new, weight, own_hit.astype(F32), msg)
    back = send_message(copies, solid, msg, edges, msg_hbm)
    nx, ny = new.shape
    nz = edges.shape[1]
    if last:
        padded = jnp.concatenate([new, jnp.zeros((LANES - nx, ny), F32)], axis=0)
        temp = sum(mul(hit_t[...], part) for part in parts(padded, 3))
        for p in range(msg.shape[0]):
            msg[p, TILE : TILE + SLOTS, :] = temp[p * SLOTS : (p + 1) * SLOTS]
        rows = pl.ds(TILE + nz, SLOTS)
        back.append(copies.start(msg.at[:, pl.ds(TILE, SLOTS), :], msg_hbm.at[:, rows, :]))
    sub, lane = iota((nx, ny), 0), iota((nx, ny), 1)
    sub_z, lane_z = iota((nz, ny), 0), iota((nz, ny), 1)

    def ends_of(rows):
        both = jnp.where(lane_z < nz, rows[:, 0:1], rows[:, ny - 1 : ny])
        both = jnp.where((lane_z % nz == sub_z) & (lane_z < 2 * nz), both, 0.0)
        return jnp.sum(both, axis=0, keepdims=True)

    value = plain[...] + jnp.where(sub == 0, ends_of(north), 0.0)
    value = value + jnp.where(sub == nx - 1, ends_of(south), 0.0)
    cols[...] = jnp.where(lane % nz == 0, pick(new, jnp.where(lane < nz, 0, ny - 1)), value)
    back.append(copies.start(cols, cols_hbm))
    for copy in back:
        copy.wait()


def final_kernel(
    got_hbm, solid_hbm, place_hbm, cond_hbm, index, scan, hit, reply, out_hbm, coolant_hbm,
    got, edges, temps, place, cond, solid, coolant, sems,
):
    copies = Copies(sems)
    nz, nx = out_hbm.shape[0], out_hbm.shape[1]
    inner = pl.ds(8, nx)
    first, *then = take_message(copies, got_hbm, got, edges)
    whole = copies.start(solid_hbm, solid)
    rows = pl.ds(TILE + nz, SLOTS)
    then += [copies.start(got_hbm.at[:, rows, :], temps), copies.start(place_hbm, place)]
    then += load_segments(copies, cond_hbm, cond)
    first.wait()
    enter = entering(got, index, scan)
    carry = hosted(enter, index)
    for copy in [whole, *then]:
        copy.wait()
    add_outer_rows(solid, edges)
    solid[1, inner, :] = new_bottom(carry, solid[1, inner, :], hit[...], reply)
    back = [copies.start(solid.at[pl.ds(1, nz), inner, :], out_hbm)]
    n_flow = got.shape[0]
    stacked = temps[...].reshape(n_flow * SLOTS, LANES)
    temp = sum(mul(place[...], part) for part in parts(stacked, 3))
    segs = temp.shape[0]
    lane = iota((segs, LANES), 1)
    gain = jnp.exp(-cond[...].reshape(segs, LANES))
    shift = (1.0 - gain) * temp
    for step in range(7):
        width = 1 << step
        shift = shift + jnp.where(lane >= width, gain * pltpu.roll(shift, width, 1), 0.0)
        gain = gain * jnp.where(lane >= width, pltpu.roll(gain, width, 1), 1.0)
    own = iota((n_flow, LANES), 0) == lax.axis_index("flow")
    line = jnp.concatenate(
        [jnp.sum(jnp.where(own, part, 0.0), axis=0, keepdims=True) for part in enter], axis=1
    )
    same = iota((segs, segs), 0) == iota((segs, segs), 1)
    start = jnp.sum(jnp.where(same, line, 0.0), axis=1, keepdims=True)
    coolant[...] = (shift + gain * start).reshape(coolant.shape)
    for s in range(coolant.shape[1]):
        target = coolant_hbm.at[:, pl.ds(s * LANES, LANES)]
        back.append(copies.start(coolant.at[:, s, :], target))
    for copy in back:
        copy.wait()


def body(solid_start, heat_gen, conductance, heat_capacity, inlet_temp, wall_owner, wall_row):
    n_flow, n_span = lax.axis_size("flow"), lax.axis_size("span")
    nz, nx, ny = solid_start.shape
    channels, stations = conductance.shape
    segs = wall_owner.shape[0]
    slots = n_flow * SLOTS
    const = jnp.pad(
        jnp.stack([heat_capacity, inlet_temp]), ((0, TILE - 2), (0, LANES - channels))
    )

    def beside_span(cols):
        up = [(i, (i + 1) % n_span) for i in range(n_span)]
        down = [(i, (i - 1) % n_span) for i in range(n_span)]
        return lax.ppermute(cols, "span", up), lax.ppermute(cols, "span", down)

    def exchange(message):
        return lax.all_to_all(message, "flow", 0, 0, tiled=True)

    lines = spec((segs // LANES, LANES), I32)
    split = spec((channels, segs // channels, LANES))
    layer, edges_spec = spec((nx, ny)), spec((2, nz, ny))
    block = spec((nz, nx, ny))
    pay_spec, place_spec = spec((n_flow, SLOTS + TILE, LANES)), spec((segs, slots), BF16)
    pay, place = call(
        source_kernel,
        (wall_owner.reshape(lines.shape), wall_row.reshape(lines.shape), conductance),
        (pay_spec, place_spec),
        (lines, lines, split, pay_spec, place_spec),
        20,
    )
    got = exchange(pay)
    room = spec((nz + 2, nx + 16, ny))
    solid, heat, cols = call(
        outer_kernel, (solid_start, heat_gen), (room, block, layer), (layer,), 3, held_out=(0, 1)
    )
    hit_spec, hit_t_spec = spec((nx, slots), BF16), spec((slots, LANES), BF16)
    reply_spec, weight_spec = spec((2, slots, LANES), BF16), spec((2, LANES, slots), BF16)
    swell_spec = spec((3, slots, LANES))
    index_spec, scan_spec = spec((5, n_flow, LANES), I32), spec((12, 2, n_flow, LANES))
    msg_spec = spec((n_flow, TILE + nz, LANES))
    long_spec = spec((n_flow, TILE + nz + SLOTS, LANES))
    short_spec, temps_spec = spec((n_flow, TILE, LANES)), spec((n_flow, SLOTS, LANES))
    constants = (
        hit_spec, hit_t_spec, reply_spec, weight_spec, swell_spec, index_spec, scan_spec, msg_spec,
    )
    hit, hit_t, reply, weight, swell, index, scan, message = call(
        owner_kernel,
        (got, solid, const),
        constants,
        (pay_spec, spec((TILE, LANES)), short_spec, edges_spec),
        5,
        held=(1,),
        held_out=range(7),
    )

    def beside(solid, cols, message):
        got = exchange(message)
        west, east = beside_span(cols)
        (sink,) = call(
            march_kernel,
            (solid, hit, hit_t, swell),
            (layer,),
            (reply_spec,),
            1,
            held=range(4),
            held_out=(0,),
            flops=2_000_000,
            nbytes=3_000_000,
        )
        solid, cols = call(
            conduct_kernel,
            (solid, heat, west, east, sink),
            (room, layer),
            (layer, layer, layer),
            3,
            held=(0, 1, 4),
            held_out=(0,),
            flops=4_000_000,
            nbytes=6_000_000,
            aliases={0: 0},
        )
        return got, solid, cols

    def step(state, last=False):
        got, solid, cols = beside(*state)
        solid, message, cols = call(
            functools.partial(after_kernel, last),
            (got, solid, cols, index, scan, hit, reply, weight, hit_t),
            (room, long_spec if last else msg_spec, layer),
            (
                short_spec, edges_spec, layer,
                spec((n_flow, TILE + SLOTS, LANES)) if last else short_spec, layer,
            ),
            9,
            held=(1, *range(3, 9)),
            held_out=(0,),
            flops=4_000_000,
            nbytes=4_000_000,
            aliases={1: 0},
        )
        return solid, cols, message

    state = lax.fori_loop(0, STEPS - 2, lambda turn, now: step(now), (solid, cols, message))
    got, solid, _ = beside(*step(state, last=True))
    return call(
        final_kernel,
        (got, solid, place, conductance, index, scan, hit, reply),
        (block, spec((channels, stations))),
        (short_spec, edges_spec, temps_spec, place_spec, split, room, split),
        7 + 2 * split.shape[1],
        held=(4, 5, 6, 7),
    )


def solution(mesh):
    placed = (
        P(None, "flow", "span"),
        P(None, "flow", "span"),
        P("span", "flow"),
        P("span"),
        P("span"),
        P(("flow", "span"), None),
        P(("flow", "span"), None),
    )
    return jax.shard_map(
        body,
        mesh=mesh,
        in_specs=placed,
        out_specs=(P(None, "flow", "span"), P("span", "flow")),
        check_vma=False,
    )
```

```python
import functools

import jax
import jax.numpy as jnp
from jax import lax
from jax.experimental import pallas as pl
from jax.experimental.pallas import tpu as pltpu
from jax.sharding import PartitionSpec as P

STEPS = 10
KAPPA = 0.16
F32 = jnp.float32
BF16 = jnp.bfloat16
I32 = jnp.int32
HI = lax.Precision.HIGHEST
LANES = 128
SLOTS = 16
TILE = 8
VMEM_LIMIT = 16 << 20
WHOLE_VMEM = 60 << 20


def iota(dims, dim):
    return lax.broadcasted_iota(I32, dims, dim)


def dot(a, b):
    return jnp.dot(a, b, precision=HI, preferred_element_type=F32)


def mul(a, b):
    return jnp.dot(a, b, preferred_element_type=F32)


def parts(x, count):
    found = []
    for _ in range(count):
        found.append(x.astype(BF16))
        x = x - found[-1].astype(F32)
    return found


def dot_t(a, b):
    return lax.dot_general(
        a, b, (((1,), (1,)), ((), ())), precision=HI, preferred_element_type=F32
    )


def pick(values, index):
    return jnp.take_along_axis(values, index, axis=1, mode="promise_in_bounds")


def spec(dims, dtype=F32):
    return jax.ShapeDtypeStruct(dims, dtype)


class Copies:
    def __init__(self, sems):
        self.sems, self.used = sems, 0

    def start(self, source, target):
        copy = pltpu.make_async_copy(source, target, self.sems.at[self.used])
        self.used += 1
        copy.start()
        return copy


def call(kernel, ins, outs, scratch, copies, held=(), held_out=(), flops=0, nbytes=0, aliases=None, limit=VMEM_LIMIT):
    return pl.pallas_call(
        kernel,
        out_shape=outs,
        in_specs=[
            pl.BlockSpec(memory_space=pltpu.VMEM if k in held else pltpu.HBM)
            for k in range(len(ins))
        ],
        out_specs=[
            pl.BlockSpec(memory_space=pltpu.VMEM if k in held_out else pltpu.HBM)
            for k in range(len(outs))
        ],
        scratch_shapes=[pltpu.VMEM(s.shape, s.dtype) for s in scratch]
        + [pltpu.SemaphoreType.DMA((copies,))],
        compiler_params=pltpu.CompilerParams(vmem_limit_bytes=limit),
        cost_estimate=pl.CostEstimate(flops=flops, bytes_accessed=nbytes, transcendentals=0),
        input_output_aliases=aliases or {},
    )(*ins)


def load_segments(copies, cond_hbm, cond):
    return [
        copies.start(cond_hbm.at[:, pl.ds(s * LANES, LANES)], cond.at[:, s, :])
        for s in range(cond.shape[1])
    ]


def source_kernel(
    owner_hbm, row_hbm, cond_hbm, pay_hbm, place_hbm, owner, row, cond, pay, place, sems
):
    copies = Copies(sems)
    first = [copies.start(owner_hbm, owner), copies.start(row_hbm, row)]
    later = load_segments(copies, cond_hbm, cond)
    for copy in first:
        copy.wait()
    segs = owner.shape[0] * LANES
    n_flow = pay.shape[0]
    slots = n_flow * SLOTS
    sub, lane = iota((segs, segs), 0), iota((segs, segs), 1)
    own_row = jnp.concatenate([owner[0:1, :], owner[1:2, :]], axis=1)
    wall_row = jnp.concatenate([row[0:1, :], row[1:2, :]], axis=1)

    def column(line):
        return jnp.sum(jnp.where(sub == lane, line, 0).astype(F32), axis=1, keepdims=True)

    own_col = column(own_row).astype(I32)
    same = own_col == own_row
    rank_row = jnp.sum((same & (sub < lane)).astype(F32), axis=0, keepdims=True).astype(I32)
    rank_col = jnp.sum((same & (lane < sub)).astype(F32), axis=1, keepdims=True).astype(I32)
    slot_row = own_row * SLOTS + rank_row
    slot_col = own_col * SLOTS + rank_col
    place[...] = (iota((segs, slots), 1) == slot_col).astype(F32).astype(BF16)
    out = copies.start(place, place_hbm)
    lanes = iota((segs, LANES), 1)
    value = jnp.where(lanes < SLOTS, column(wall_row).astype(I32), iota((segs, LANES), 0))
    value = jnp.where((lanes < 2 * SLOTS) & (lanes % SLOTS == rank_col), value, 0)
    held = (iota((n_flow, segs), 0) == own_row).astype(F32)
    meta = mul(held.astype(BF16), value.astype(F32).astype(BF16))
    for copy in later:
        copy.wait()
    cond_rows = cond[...].reshape(segs, LANES)
    chosen = (iota((slots, segs), 0) == slot_row).astype(F32).astype(BF16)
    moved = sum(mul(chosen, part) for part in parts(cond_rows, 3))
    total = dot_t(jnp.ones((TILE, LANES), F32), cond_rows)[0:1]
    sub8 = iota((TILE, LANES), 0)
    common = jnp.zeros((TILE, LANES), F32)
    slot_f = slot_row.astype(F32)
    for half in range(2):
        cols = slice(half * LANES, (half + 1) * LANES)
        common = jnp.where(sub8 == 1 + half, slot_f[:, cols], common)
        common = jnp.where(sub8 == 3 + half, total[:, cols], common)
    for p in range(n_flow):
        pay[p, 0:SLOTS, :] = moved[p * SLOTS : (p + 1) * SLOTS]
        pay[p, SLOTS : SLOTS + TILE, :] = jnp.where(sub8 == 0, meta[p : p + 1], common)
    back = copies.start(pay, pay_hbm)
    out.wait()
    back.wait()


def outer_kernel(solid_hbm, solid, cols, sems):
    copies = Copies(sems)
    nz, nx, ny = solid_hbm.shape
    inner = pl.ds(8, nx)
    copies.start(solid_hbm, solid.at[pl.ds(1, nz), inner, :]).wait()
    lane = iota((nx, ny), 1)
    ends = jnp.where(lane < nz, 0, ny - 1)
    solid[0, inner, :] = jnp.zeros((nx, ny), F32)
    solid[nz + 1, inner, :] = jnp.zeros((nx, ny), F32)
    solid[pl.ds(1, nz), 7, :] = jnp.zeros((nz, ny), F32)
    solid[pl.ds(1, nz), 8 + nx, :] = jnp.zeros((nz, ny), F32)
    unroll = 4

    def some(i, found):
        for j in range(unroll):
            z = i * unroll + j
            found = jnp.where(lane % nz == z, pick(solid[z + 1, inner, :], ends), found)
        return found

    cols[...] = lax.fori_loop(0, nz // unroll, some, jnp.zeros((nx, ny), F32))


def owner_kernel(
    got_hbm, solid, const_hbm,
    hit, hit_t, reply, weight, swell, scan, msg_hbm,
    got, const, msg, edges, sems,
):
    copies = Copies(sems)
    for copy in [copies.start(got_hbm, got), copies.start(const_hbm, const)]:
        copy.wait()
    bottom = solid[1, pl.ds(8, hit.shape[0]), :]
    n_flow = got.shape[0]
    slots = n_flow * SLOTS
    block_rows = bottom.shape[0]
    meta = got[:, SLOTS, :]
    lane8, sub8 = iota((TILE, LANES), 1), iota((TILE, LANES), 0)
    mine = lane8 // SLOTS == sub8
    hits, caps = [], []
    n_grp = n_flow // TILE
    rows = iota((LANES, LANES), 0)
    cap8 = jnp.broadcast_to(const[0:1, :], (TILE, LANES))
    for g in range(n_grp):
        part = meta[g * TILE : (g + 1) * TILE]
        row = jnp.sum(jnp.where(mine, pick(part, lane8 % SLOTS), 0.0), axis=0, keepdims=True)
        seg = jnp.where(mine, pick(part, SLOTS + lane8 % SLOTS), 0.0)
        seg = jnp.sum(seg, axis=0, keepdims=True).astype(I32)
        seg8 = jnp.broadcast_to(seg, (TILE, LANES))
        scan[14, 0, g * TILE : (g + 1) * TILE, :] = seg8.astype(F32)
        cap = pick(cap8, seg8 // 16)[0:1]
        hits.append((rows == row.astype(I32)).astype(F32))
        caps.append(jnp.transpose(jnp.broadcast_to(cap, (LANES, LANES))))
    all_hit = jnp.concatenate(hits, axis=1)
    own_hit = all_hit[0:block_rows]
    hit[...] = own_hit.astype(BF16)
    cond = got[:, 0:SLOTS, :].reshape(slots, LANES)
    sub_t, lane_t = iota((LANES, LANES), 0), iota((LANES, LANES), 1)
    after = sum(
        mul(part, (sub_t > lane_t).astype(F32).astype(BF16)) for part in parts(cond, 3)
    )
    decay = jnp.exp(-cond)
    own_rate = 1.0 - decay
    halves = parts(jnp.transpose(own_rate * jnp.exp(-after)), 2)
    for half in range(2):
        weight[half] = halves[half]
    write_shifts(bottom, weight, own_hit, msg)
    back = send_message(copies, solid, msg, edges, msg_hbm)
    hit_t[...] = jnp.transpose(all_hit).astype(BF16)
    own_caprate = own_rate * jnp.concatenate(caps, axis=0)
    ahead = sum(
        mul(part, (sub_t < lane_t).astype(F32).astype(BF16)) for part in parts(cond, 3)
    )
    halves = parts(own_caprate * jnp.exp(-ahead), 2)
    for half in range(2):
        reply[half] = halves[half]
    middle = jnp.sum(
        jnp.where(iota((slots, LANES), 1) < LANES // 2, cond, 0.0), axis=1, keepdims=True
    )
    swell[0] = own_rate * jnp.exp(ahead + cond - middle)
    swell[1] = jnp.exp(middle - ahead)
    swell[2] = own_caprate
    scan[14, 1] = jnp.zeros((n_flow, LANES), F32)
    lane_f, sub_f = iota((n_flow, LANES), 1), iota((n_flow, LANES), 0)
    inlet = jnp.broadcast_to(const[1:2, :], (n_flow, LANES))
    for half in range(2):
        slot = got[:, SLOTS + 1 + half, :].astype(I32)
        scan[12, half] = ((sub_f % TILE) * SLOTS + slot % SLOTS).astype(F32)
        scan[13, half] = (slot // SLOTS).astype(F32)
        gain = jnp.exp(-got[:, SLOTS + 3 + half, :])
        inner = lane_f % 16
        for step in range(4):
            width = 1 << step
            scan[step, half] = jnp.where(inner >= width, gain, 0.0)
            gain = gain * jnp.where(inner >= width, pltpu.roll(gain, width, 1), 1.0)
        scan[10, half] = jnp.where(inner == 0, 1.0, pltpu.roll(gain, 1, 1))
        scan[9, half] = gain
        for step in range(5):
            width = 1 << step
            scan[4 + step, half] = jnp.where(sub_f >= width, gain, 0.0)
            gain = gain * jnp.where(sub_f >= width, pltpu.roll(gain, width, 0), 1.0)
        scan[11, half] = pick(inlet, lane_f // 16 + 8 * half)
    for copy in back:
        copy.wait()


def write_shifts(bottom, weight, hit, msg):
    high, low = parts(bottom, 2)
    ends = mul(high, weight[0]) + (mul(high, weight[1]) + mul(low, weight[0]))
    ends = jnp.sum(ends * hit, axis=0, keepdims=True)
    sub8 = iota((TILE, LANES), 0)
    tile = jnp.zeros((TILE, LANES), F32)
    for g in range(ends.shape[1] // LANES):
        tile = jnp.where(sub8 == g, ends[:, g * LANES : (g + 1) * LANES], tile)
    for p in range(msg.shape[0]):
        msg[p, 0:TILE, :] = tile


def send_message(copies, solid, msg, edges, msg_hbm):
    n_flow, me = msg.shape[0], lax.axis_index("flow")
    nz, nx = edges.shape[1], solid.shape[1] - 16
    edges[0] = solid[pl.ds(1, nz), 8, :]
    edges[1] = solid[pl.ds(1, nz), 7 + nx, :]
    rows = pl.ds(TILE, nz)
    return [
        copies.start(edges.at[0], msg_hbm.at[lax.rem(me + n_flow - 1, n_flow), rows, :]),
        copies.start(edges.at[1], msg_hbm.at[lax.rem(me + 1, n_flow), rows, :]),
        copies.start(msg.at[:, pl.ds(0, TILE), :], msg_hbm.at[:, pl.ds(0, TILE), :]),
    ]


def add_outer_rows(solid, got):
    n_flow, me = lax.axis_size("flow"), lax.axis_index("flow")
    nz, nx = solid.shape[0] - 2, solid.shape[1] - 16
    rows = pl.ds(TILE, nz)
    north = got[lax.rem(me + n_flow - 1, n_flow), rows, :]
    south = got[lax.rem(me + 1, n_flow), rows, :]
    north = jnp.where(me > 0, KAPPA * north, 0.0)
    south = jnp.where(me < n_flow - 1, KAPPA * south, 0.0)
    layers = pl.ds(1, nz)
    solid[layers, 8, :] = solid[layers, 8, :] + north
    solid[layers, 7 + nx, :] = solid[layers, 7 + nx, :] + south
    return north, south


def march_kernel(part, solid, hit, hit_t, swell, *rest):
    *earlier_sink, sink, flux, _ = rest
    slots = flux.shape[1]
    piece = slots // 2
    nx, ny = sink.shape
    bottom = solid[1, pl.ds(8, nx), :]
    padded = jnp.concatenate([bottom, jnp.zeros((LANES - nx, ny), F32)], axis=0)
    wide = jnp.concatenate(parts(padded, 3), axis=1)
    earlier = (iota((LANES, LANES), 0) < iota((LANES, LANES), 1)).astype(F32).astype(BF16)
    for i in range(2):
        rows = pl.ds(part * slots + i * piece, piece)
        to = pl.ds(i * piece, piece)
        triple = mul(hit_t[rows, :], wide)
        temp = (triple[:, 0:ny] + triple[:, ny : 2 * ny]) + triple[:, 2 * ny :]
        high, low = parts(swell[0, rows, :] * temp, 2)
        before = swell[1, rows, :] * (mul(high, earlier) + mul(low, earlier))
        high, low = parts(swell[2, rows, :] * (temp - before), 2)
        flux[0, to, :] = high
        flux[1, to, :] = low
    own = hit[:, part * slots : (part + 1) * slots]
    total = mul(own, flux[0]) + mul(own, flux[1])
    for other in earlier_sink:
        total = total + other[...]
    sink[...] = total


def conduct_kernel(
    old, heat, west, east, sink, solid, cols, sems
):
    del old
    nz, nx, ny = heat.shape
    del sems
    inner = pl.ds(8, nx)
    lot, n_span = lax.axis_index("span"), lax.axis_size("span")
    lane = iota((nx, ny), 1)
    border = (lane == 0) | (lane == ny - 1)
    ends = jnp.where(lane < nz, 0, ny - 1)
    halo = jnp.where((lane < nz) & (lot < n_span - 1), east[...], 0.0)
    halo = jnp.where((lane >= nz) & (lot > 0), west[...], halo)
    unroll = 4

    def some(i, state):
        found, low = state
        for j in range(unroll):
            z = i * unroll + j
            mid = solid[z + 1, inner, :]
            side = pick(halo, jnp.where(lane == 0, nz, 0) + z)
            right, left = pltpu.roll(mid, 1, 1), pltpu.roll(mid, ny - 1, 1)
            across = jnp.where(border, side + jnp.where(lane == 0, left, right), left + right)
            total = across + (solid[z + 1, pl.ds(7, nx), :] + solid[z + 1, pl.ds(9, nx), :])
            total = total + (low + solid[z + 2, inner, :])
            new = mid + KAPPA * (total - 6.0 * mid) + heat[z]
            solid[z + 1, inner, :] = new
            found = jnp.where(lane % nz == z, pick(new, ends), found)
            low = mid
        return found, low

    zero = jnp.zeros((nx, ny), F32)
    cols[...], _ = lax.fori_loop(0, nz // unroll, some, (zero, zero))
    solid[1, inner, :] = solid[1, inner, :] - sink[...]


def take_scan(copies, scan_hbm, scan):
    places, gains = pl.ds(12, 3), pl.ds(0, 12)
    return [
        copies.start(scan_hbm.at[rows], scan.at[rows]) for rows in (places, gains)
    ]


def entering(got, scan, gains):
    n_flow = got.shape[0]
    ends = [[], []]
    for g in range(n_flow // TILE):
        rows = slice(g * TILE, (g + 1) * TILE)
        lanes = [scan[12, half, rows, :].astype(I32) for half in range(2)]
        origin = [scan[13, half, rows, :] for half in range(2)]
        acc = [jnp.zeros((TILE, LANES), F32) for _ in range(2)]
        for o in range(n_flow):
            line = jnp.broadcast_to(got[o, g : g + 1, :], (TILE, LANES))
            for half in range(2):
                acc[half] = jnp.where(origin[half] == float(o), pick(line, lanes[half]), acc[half])
        for half in range(2):
            ends[half].append(acc[half])
    gains.wait()
    result = []
    sub, lane = iota((n_flow, LANES), 0), iota((n_flow, LANES), 1)
    for half in range(2):
        x = jnp.concatenate(ends[half], axis=0)
        for step in range(4):
            x = x + scan[step, half] * pltpu.roll(x, 1 << step, 1)
        inlet = scan[11, half]
        y = jnp.where(sub == 0, x + scan[9, half] * inlet, x)
        for step in range(5):
            y = y + scan[4 + step, half] * pltpu.roll(y, 1 << step, 0)
        carry = jnp.where(sub == 0, inlet, pltpu.roll(y, 1, 0))
        carry = pick(carry, lane // 16 * 16 + 15)
        earlier = jnp.where(lane % 16 == 0, 0.0, pltpu.roll(x, 1, 1))
        result.append(earlier + scan[10, half] * carry)
    return result


def hosted(enter, scan):
    lane8, sub8 = iota((TILE, LANES), 1), iota((TILE, LANES), 0)
    found = []
    for g in range(enter[0].shape[0] // TILE):
        rows = slice(g * TILE, (g + 1) * TILE)
        seg = scan[14, 0, rows, :].astype(I32)
        low, high = (pick(enter[half][rows], seg % LANES) for half in range(2))
        value = jnp.where(lane8 // SLOTS == sub8, jnp.where(seg < LANES, low, high), 0.0)
        found.append(jnp.sum(value, axis=0, keepdims=True))
    return jnp.concatenate(found, axis=1)


def new_bottom(carry, base, hit, reply):
    high, low = parts(carry, 2)
    high, low = hit * high, hit * low
    return base + (mul(high, reply[0]) + (mul(high, reply[1]) + mul(low, reply[0])))


def after_kernel(
    last,
    got, old, plain, scan_hbm, hit, reply_hbm, weight_hbm, hit_t,
    solid, msg_hbm, cols,
    scan, edges, msg, reply, weight, sems,
):
    del old
    copies = Copies(sems)
    places, gains = take_scan(copies, scan_hbm, scan)
    come = [copies.start(reply_hbm, reply), copies.start(weight_hbm, weight)]
    north, south = add_outer_rows(solid, got)
    places.wait()
    carry = hosted(entering(got, scan, gains), scan)
    own_hit = hit[...]
    nx = own_hit.shape[0]
    inner = pl.ds(8, nx)
    come[0].wait()
    new = new_bottom(carry, solid[1, inner, :], own_hit, reply)
    solid[1, inner, :] = new
    come[1].wait()
    write_shifts(new, weight, own_hit.astype(F32), msg)
    back = send_message(copies, solid, msg, edges, msg_hbm)
    nx, ny = new.shape
    nz = edges.shape[1]
    if last:
        padded = jnp.concatenate([new, jnp.zeros((LANES - nx, ny), F32)], axis=0)
        temp = sum(mul(hit_t[...], part) for part in parts(padded, 3))
        for p in range(msg.shape[0]):
            msg[p, TILE : TILE + SLOTS, :] = temp[p * SLOTS : (p + 1) * SLOTS]
        rows = pl.ds(TILE + nz, SLOTS)
        back.append(copies.start(msg.at[:, pl.ds(TILE, SLOTS), :], msg_hbm.at[:, rows, :]))
    sub, lane = iota((nx, ny), 0), iota((nx, ny), 1)
    sub_z, lane_z = iota((nz, ny), 0), iota((nz, ny), 1)

    def ends_of(rows):
        both = jnp.where(lane_z < nz, rows[:, 0:1], rows[:, ny - 1 : ny])
        both = jnp.where((lane_z % nz == sub_z) & (lane_z < 2 * nz), both, 0.0)
        return jnp.sum(both, axis=0, keepdims=True)

    value = plain[...] + jnp.where(sub == 0, ends_of(north), 0.0)
    value = value + jnp.where(sub == nx - 1, ends_of(south), 0.0)
    cols[...] = jnp.where(lane % nz == 0, pick(new, jnp.where(lane < nz, 0, ny - 1)), value)
    for copy in back:
        copy.wait()


def final_kernel(
    got, old, place_hbm, cond_hbm, scan_hbm, hit, reply_hbm, solid, out_hbm, coolant_hbm,
    scan, place, cond, reply, coolant, sems,
):
    copies = Copies(sems)
    nz, nx = out_hbm.shape[0], out_hbm.shape[1]
    inner = pl.ds(8, nx)
    del old
    places, gains = take_scan(copies, scan_hbm, scan)
    come = copies.start(reply_hbm, reply)
    then = [copies.start(place_hbm, place), *load_segments(copies, cond_hbm, cond)]
    add_outer_rows(solid, got)
    upper = pl.ds(2, nz - 1)
    back = [copies.start(solid.at[upper, inner, :], out_hbm.at[pl.ds(1, nz - 1)])]
    places.wait()
    enter = entering(got, scan, gains)
    carry = hosted(enter, scan)
    come.wait()
    solid[1, inner, :] = new_bottom(carry, solid[1, inner, :], hit[...], reply)
    back.append(copies.start(solid.at[1, inner, :], out_hbm.at[0]))
    for copy in then:
        copy.wait()
    n_flow = got.shape[0]
    stacked = got[:, TILE + nz :, :].reshape(n_flow * SLOTS, LANES)
    temp = sum(mul(place[...], part) for part in parts(stacked, 3))
    segs = temp.shape[0]
    lane = iota((segs, LANES), 1)
    gain = jnp.exp(-cond[...].reshape(segs, LANES))
    shift = (1.0 - gain) * temp
    for step in range(7):
        width = 1 << step
        shift = shift + jnp.where(lane >= width, gain * pltpu.roll(shift, width, 1), 0.0)
        gain = gain * jnp.where(lane >= width, pltpu.roll(gain, width, 1), 1.0)
    own = iota((n_flow, LANES), 0) == lax.axis_index("flow")
    line = jnp.concatenate(
        [jnp.sum(jnp.where(own, part, 0.0), axis=0, keepdims=True) for part in enter], axis=1
    )
    same = iota((segs, segs), 0) == iota((segs, segs), 1)
    start = jnp.sum(jnp.where(same, line, 0.0), axis=1, keepdims=True)
    coolant[...] = (shift + gain * start).reshape(coolant.shape)
    for s in range(coolant.shape[1]):
        target = coolant_hbm.at[:, pl.ds(s * LANES, LANES)]
        back.append(copies.start(coolant.at[:, s, :], target))
    for copy in back:
        copy.wait()


def body(solid_start, heat_gen, conductance, heat_capacity, inlet_temp, wall_owner, wall_row):
    n_flow, n_span = lax.axis_size("flow"), lax.axis_size("span")
    nz, nx, ny = solid_start.shape
    channels, stations = conductance.shape
    segs = wall_owner.shape[0]
    slots = n_flow * SLOTS
    const = jnp.pad(
        jnp.stack([heat_capacity, inlet_temp]), ((0, TILE - 2), (0, LANES - channels))
    )

    def exchange(message):
        return lax.all_to_all(message, "flow", 0, 0, tiled=True)

    lines = spec((segs // LANES, LANES), I32)
    split = spec((channels, segs // channels, LANES))
    layer, edges_spec = spec((nx, ny)), spec((2, nz, ny))
    block = spec((nz, nx, ny))
    pay_spec, place_spec = spec((n_flow, SLOTS + TILE, LANES)), spec((segs, slots), BF16)
    pay, place = call(
        source_kernel,
        (wall_owner.reshape(lines.shape), wall_row.reshape(lines.shape), conductance),
        (pay_spec, place_spec),
        (lines, lines, split, pay_spec, place_spec),
        20,
        limit=WHOLE_VMEM,
    )
    got = exchange(pay)
    room = spec((nz + 2, nx + 16, ny))
    solid, cols = call(
        outer_kernel, (solid_start,), (room, layer), (), 1, held_out=(0, 1), limit=WHOLE_VMEM
    )
    hit_spec, hit_t_spec = spec((nx, slots), BF16), spec((slots, LANES), BF16)
    reply_spec, weight_spec = spec((2, slots, LANES), BF16), spec((2, LANES, slots), BF16)
    swell_spec = spec((3, slots, LANES))
    scan_spec = spec((15, 2, n_flow, LANES))
    msg_spec = spec((n_flow, TILE + nz, LANES))
    long_spec = spec((n_flow, TILE + nz + SLOTS, LANES))
    short_spec = spec((n_flow, TILE, LANES))
    constants = (
        hit_spec, hit_t_spec, reply_spec, weight_spec, swell_spec, scan_spec, msg_spec,
    )
    hit, hit_t, reply, weight, swell, scan, message = call(
        owner_kernel,
        (got, solid, const),
        constants,
        (pay_spec, spec((TILE, LANES)), short_spec, edges_spec),
        5,
        held=(1,),
        held_out=range(6),
    )

    def march(part, *operands):
        (sink,) = call(
            functools.partial(march_kernel, part),
            operands,
            (layer,),
            (spec((2, slots // 2, LANES), BF16),),
            1,
            held=range(len(operands)),
            held_out=(0,),
            flops=1_000_000,
            nbytes=1_500_000,
        )
        return sink

    def beside(solid, cols, message):
        got = exchange(message)
        up = [(i, (i + 1) % n_span) for i in range(n_span)]
        down = [(i, (i - 1) % n_span) for i in range(n_span)]
        west = lax.ppermute(cols, "span", up)
        sink = march(0, solid, hit, hit_t, swell)
        cols, sink = lax.optimization_barrier((cols, sink))
        east = lax.ppermute(cols, "span", down)
        west, sink = lax.optimization_barrier((west, sink))
        sink = march(1, solid, hit, hit_t, swell, sink)
        solid, cols = call(
            conduct_kernel,
            (solid, heat_gen, west, east, sink),
            (room, layer),
            (),
            1,
            held=range(5),
            held_out=(0, 1),
            flops=4_000_000,
            nbytes=6_000_000,
            aliases={0: 0},
        )
        return got, solid, cols

    def step(state, last=False):
        got, solid, cols = beside(*state)
        solid, message, cols = call(
            functools.partial(after_kernel, last),
            (got, solid, cols, scan, hit, reply, weight, hit_t),
            (room, long_spec if last else msg_spec, layer),
            (
                scan_spec,
                edges_spec, spec((n_flow, TILE + SLOTS, LANES)) if last else short_spec,
                reply_spec, weight_spec,
            ),
            8,
            held=(0, 1, 2, 4, 7),
            held_out=(0, 2),
            flops=4_000_000,
            nbytes=4_000_000,
            aliases={1: 0},
        )
        return solid, cols, message

    state = lax.fori_loop(0, STEPS - 2, lambda turn, now: step(now), (solid, cols, message))
    got, solid, _ = beside(*step(state, last=True))
    _, solid, coolant = call(
        final_kernel,
        (got, solid, place, conductance, scan, hit, reply),
        (room, block, spec((channels, stations))),
        (scan_spec, place_spec, split, reply_spec, split),
        6 + 2 * split.shape[1],
        held=(0, 1, 5),
        held_out=(0,),
        aliases={1: 0},
    )
    return solid, coolant


def solution(mesh):
    placed = (
        P(None, "flow", "span"),
        P(None, "flow", "span"),
        P("span", "flow"),
        P("span"),
        P("span"),
        P(("flow", "span"), None),
        P(("flow", "span"), None),
    )
    return jax.shard_map(
        body,
        mesh=mesh,
        in_specs=placed,
        out_specs=(P(None, "flow", "span"), P("span", "flow")),
        check_vma=False,
    )
```

```python
import functools

import jax
import jax.numpy as jnp
from jax import lax
from jax.experimental import pallas as pl
from jax.experimental.pallas import tpu as pltpu
from jax.sharding import PartitionSpec as P

STEPS = 10
KAPPA = 0.16
F32 = jnp.float32
BF16 = jnp.bfloat16
I32 = jnp.int32
HI = lax.Precision.HIGHEST
LANES = 128
SLOTS = 16
TILE = 8
VMEM_LIMIT = 16 << 20
WHOLE_VMEM = 60 << 20


def iota(dims, dim):
    return lax.broadcasted_iota(I32, dims, dim)


def dot(a, b):
    return jnp.dot(a, b, precision=HI, preferred_element_type=F32)


def mul(a, b):
    return jnp.dot(a, b, preferred_element_type=F32)


def parts(x, count):
    found = []
    for _ in range(count):
        found.append(x.astype(BF16))
        x = x - found[-1].astype(F32)
    return found


def dot_t(a, b):
    return lax.dot_general(
        a, b, (((1,), (1,)), ((), ())), precision=HI, preferred_element_type=F32
    )


def pick(values, index):
    return jnp.take_along_axis(values, index, axis=1, mode="promise_in_bounds")


def spec(dims, dtype=F32):
    return jax.ShapeDtypeStruct(dims, dtype)


class Copies:
    def __init__(self, sems):
        self.sems, self.used = sems, 0

    def start(self, source, target):
        copy = pltpu.make_async_copy(source, target, self.sems.at[self.used])
        self.used += 1
        copy.start()
        return copy


def call(kernel, ins, outs, scratch, copies, held=(), held_out=(), flops=0, nbytes=0, aliases=None, limit=VMEM_LIMIT):
    return pl.pallas_call(
        kernel,
        out_shape=outs,
        in_specs=[
            pl.BlockSpec(memory_space=pltpu.VMEM if k in held else pltpu.HBM)
            for k in range(len(ins))
        ],
        out_specs=[
            pl.BlockSpec(memory_space=pltpu.VMEM if k in held_out else pltpu.HBM)
            for k in range(len(outs))
        ],
        scratch_shapes=[pltpu.VMEM(s.shape, s.dtype) for s in scratch]
        + [pltpu.SemaphoreType.DMA((copies,))],
        compiler_params=pltpu.CompilerParams(vmem_limit_bytes=limit),
        cost_estimate=pl.CostEstimate(flops=flops, bytes_accessed=nbytes, transcendentals=0),
        input_output_aliases=aliases or {},
    )(*ins)


def load_segments(copies, cond_hbm, cond):
    return [
        copies.start(cond_hbm.at[:, pl.ds(s * LANES, LANES)], cond.at[:, s, :])
        for s in range(cond.shape[1])
    ]


def source_kernel(
    owner_hbm, row_hbm, cond_hbm, pay_hbm, place_hbm, owner, row, cond, pay, place, sems
):
    copies = Copies(sems)
    first = [copies.start(owner_hbm, owner), copies.start(row_hbm, row)]
    later = load_segments(copies, cond_hbm, cond)
    for copy in first:
        copy.wait()
    segs = owner.shape[0] * LANES
    n_flow = pay.shape[0]
    slots = n_flow * SLOTS
    sub, lane = iota((segs, segs), 0), iota((segs, segs), 1)
    own_row = jnp.concatenate([owner[0:1, :], owner[1:2, :]], axis=1)
    wall_row = jnp.concatenate([row[0:1, :], row[1:2, :]], axis=1)

    def column(line):
        return jnp.sum(jnp.where(sub == lane, line, 0).astype(F32), axis=1, keepdims=True)

    own_col = column(own_row).astype(I32)
    same = own_col == own_row
    rank_row = jnp.sum((same & (sub < lane)).astype(F32), axis=0, keepdims=True).astype(I32)
    rank_col = jnp.sum((same & (lane < sub)).astype(F32), axis=1, keepdims=True).astype(I32)
    slot_row = own_row * SLOTS + rank_row
    slot_col = own_col * SLOTS + rank_col
    place[...] = (iota((segs, slots), 1) == slot_col).astype(F32).astype(BF16)
    out = copies.start(place, place_hbm)
    lanes = iota((segs, LANES), 1)
    value = jnp.where(lanes < SLOTS, column(wall_row).astype(I32), iota((segs, LANES), 0))
    value = jnp.where((lanes < 2 * SLOTS) & (lanes % SLOTS == rank_col), value, 0)
    held = (iota((n_flow, segs), 0) == own_row).astype(F32)
    meta = mul(held.astype(BF16), value.astype(F32).astype(BF16))
    for copy in later:
        copy.wait()
    cond_rows = cond[...].reshape(segs, LANES)
    chosen = (iota((slots, segs), 0) == slot_row).astype(F32).astype(BF16)
    moved = sum(mul(chosen, part) for part in parts(cond_rows, 3))
    total = dot_t(jnp.ones((TILE, LANES), F32), cond_rows)[0:1]
    sub8 = iota((TILE, LANES), 0)
    common = jnp.zeros((TILE, LANES), F32)
    slot_f = slot_row.astype(F32)
    for half in range(2):
        cols = slice(half * LANES, (half + 1) * LANES)
        common = jnp.where(sub8 == 1 + half, slot_f[:, cols], common)
        common = jnp.where(sub8 == 3 + half, total[:, cols], common)
    for p in range(n_flow):
        pay[p, 0:SLOTS, :] = moved[p * SLOTS : (p + 1) * SLOTS]
        pay[p, SLOTS : SLOTS + TILE, :] = jnp.where(sub8 == 0, meta[p : p + 1], common)
    back = copies.start(pay, pay_hbm)
    out.wait()
    back.wait()


def outer_kernel(solid_hbm, solid, cols, sems):
    copies = Copies(sems)
    nz, nx, ny = solid_hbm.shape
    inner = pl.ds(0, nx)
    copies.start(solid_hbm, solid.at[pl.ds(1, nz), inner, :]).wait()
    lane = iota((nx, ny), 1)
    ends = jnp.where(lane < nz, 0, ny - 1)
    solid[0, inner, :] = jnp.zeros((nx, ny), F32)
    solid[nz + 1, inner, :] = jnp.zeros((nx, ny), F32)
    unroll = 4

    def some(i, found):
        for j in range(unroll):
            z = i * unroll + j
            found = jnp.where(lane % nz == z, pick(solid[z + 1, inner, :], ends), found)
        return found

    cols[...] = lax.fori_loop(0, nz // unroll, some, jnp.zeros((nx, ny), F32))


def owner_kernel(
    got_hbm, solid, const_hbm,
    hit, hit_t, reply, weight, swell, scan, msg_hbm,
    got, const, msg, edges, sems,
):
    copies = Copies(sems)
    for copy in [copies.start(got_hbm, got), copies.start(const_hbm, const)]:
        copy.wait()
    bottom = solid[1]
    n_flow = got.shape[0]
    slots = n_flow * SLOTS
    block_rows = bottom.shape[0]
    meta = got[:, SLOTS, :]
    lane8, sub8 = iota((TILE, LANES), 1), iota((TILE, LANES), 0)
    mine = lane8 // SLOTS == sub8
    hits, caps = [], []
    n_grp = n_flow // TILE
    rows = iota((LANES, LANES), 0)
    cap8 = jnp.broadcast_to(const[0:1, :], (TILE, LANES))
    for g in range(n_grp):
        part = meta[g * TILE : (g + 1) * TILE]
        row = jnp.sum(jnp.where(mine, pick(part, lane8 % SLOTS), 0.0), axis=0, keepdims=True)
        seg = jnp.where(mine, pick(part, SLOTS + lane8 % SLOTS), 0.0)
        seg = jnp.sum(seg, axis=0, keepdims=True).astype(I32)
        seg8 = jnp.broadcast_to(seg, (TILE, LANES))
        scan[14, 0, g * TILE : (g + 1) * TILE, :] = seg8.astype(F32)
        cap = pick(cap8, seg8 // 16)[0:1]
        hits.append((rows == row.astype(I32)).astype(F32))
        caps.append(jnp.transpose(jnp.broadcast_to(cap, (LANES, LANES))))
    all_hit = jnp.concatenate(hits, axis=1)
    own_hit = all_hit[0:block_rows]
    hit[...] = own_hit.astype(BF16)
    cond = got[:, 0:SLOTS, :].reshape(slots, LANES)
    sub_t, lane_t = iota((LANES, LANES), 0), iota((LANES, LANES), 1)
    after = sum(
        mul(part, (sub_t > lane_t).astype(F32).astype(BF16)) for part in parts(cond, 3)
    )
    decay = jnp.exp(-cond)
    own_rate = 1.0 - decay
    halves = parts(jnp.transpose(own_rate * jnp.exp(-after)), 2)
    for half in range(2):
        weight[half] = halves[half]
    write_shifts(bottom, weight, own_hit, msg)
    back = send_message(copies, solid, msg, edges, msg_hbm)
    hit_t[...] = jnp.transpose(all_hit).astype(BF16)
    own_caprate = own_rate * jnp.concatenate(caps, axis=0)
    ahead = sum(
        mul(part, (sub_t < lane_t).astype(F32).astype(BF16)) for part in parts(cond, 3)
    )
    halves = parts(own_caprate * jnp.exp(-ahead), 2)
    for half in range(2):
        reply[half] = halves[half]
    middle = jnp.sum(
        jnp.where(iota((slots, LANES), 1) < LANES // 2, cond, 0.0), axis=1, keepdims=True
    )
    swell[0] = own_rate * jnp.exp(ahead + cond - middle)
    swell[1] = jnp.exp(middle - ahead)
    swell[2] = own_caprate
    scan[14, 1] = jnp.zeros((n_flow, LANES), F32)
    lane_f, sub_f = iota((n_flow, LANES), 1), iota((n_flow, LANES), 0)
    inlet = jnp.broadcast_to(const[1:2, :], (n_flow, LANES))
    for half in range(2):
        slot = got[:, SLOTS + 1 + half, :].astype(I32)
        scan[12, half] = ((sub_f % TILE) * SLOTS + slot % SLOTS).astype(F32)
        scan[13, half] = (slot // SLOTS).astype(F32)
        gain = jnp.exp(-got[:, SLOTS + 3 + half, :])
        inner = lane_f % 16
        for step in range(4):
            width = 1 << step
            scan[step, half] = jnp.where(inner >= width, gain, 0.0)
            gain = gain * jnp.where(inner >= width, pltpu.roll(gain, width, 1), 1.0)
        scan[10, half] = jnp.where(inner == 0, 1.0, pltpu.roll(gain, 1, 1))
        scan[9, half] = gain
        for step in range(5):
            width = 1 << step
            scan[4 + step, half] = jnp.where(sub_f >= width, gain, 0.0)
            gain = gain * jnp.where(sub_f >= width, pltpu.roll(gain, width, 0), 1.0)
        scan[11, half] = pick(inlet, lane_f // 16 + 8 * half)
    for copy in back:
        copy.wait()


def write_shifts(bottom, weight, hit, msg):
    high, low = parts(bottom, 2)
    ends = mul(high, weight[0]) + (mul(high, weight[1]) + mul(low, weight[0]))
    ends = jnp.sum(ends * hit, axis=0, keepdims=True)
    sub8 = iota((TILE, LANES), 0)
    tile = jnp.zeros((TILE, LANES), F32)
    for g in range(ends.shape[1] // LANES):
        tile = jnp.where(sub8 == g, ends[:, g * LANES : (g + 1) * LANES], tile)
    for p in range(msg.shape[0]):
        msg[p, 0:TILE, :] = tile


def send_message(copies, solid, msg, edges, msg_hbm):
    n_flow, me = msg.shape[0], lax.axis_index("flow")
    nz, nx = edges.shape[1], solid.shape[1]
    edges[0] = solid[pl.ds(1, nz), 0, :]
    edges[1] = solid[pl.ds(1, nz), nx - 1, :]
    rows = pl.ds(TILE, nz)
    return [
        copies.start(edges.at[0], msg_hbm.at[lax.rem(me + n_flow - 1, n_flow), rows, :]),
        copies.start(edges.at[1], msg_hbm.at[lax.rem(me + 1, n_flow), rows, :]),
        copies.start(msg.at[:, pl.ds(0, TILE), :], msg_hbm.at[:, pl.ds(0, TILE), :]),
    ]


def add_outer_rows(solid, got):
    n_flow, me = lax.axis_size("flow"), lax.axis_index("flow")
    nz, nx = solid.shape[0] - 2, solid.shape[1]
    rows = pl.ds(TILE, nz)
    north = got[lax.rem(me + n_flow - 1, n_flow), rows, :]
    south = got[lax.rem(me + 1, n_flow), rows, :]
    north = jnp.where(me > 0, KAPPA * north, 0.0)
    south = jnp.where(me < n_flow - 1, KAPPA * south, 0.0)
    layers = pl.ds(1, nz)
    solid[layers, 0, :] = solid[layers, 0, :] + north
    solid[layers, nx - 1, :] = solid[layers, nx - 1, :] + south
    return north, south


def march_kernel(part, solid, hit, hit_t, swell, *rest):
    *earlier_sink, sink, flux, _ = rest
    slots = flux.shape[1]
    piece = slots // 2
    nx, ny = sink.shape
    bottom = solid[1]
    padded = jnp.concatenate([bottom, jnp.zeros((LANES - nx, ny), F32)], axis=0)
    wide = jnp.concatenate(parts(padded, 3), axis=1)
    earlier = (iota((LANES, LANES), 0) < iota((LANES, LANES), 1)).astype(F32).astype(BF16)
    for i in range(2):
        rows = pl.ds(part * slots + i * piece, piece)
        to = pl.ds(i * piece, piece)
        triple = mul(hit_t[rows, :], wide)
        temp = (triple[:, 0:ny] + triple[:, ny : 2 * ny]) + triple[:, 2 * ny :]
        high, low = parts(swell[0, rows, :] * temp, 2)
        before = swell[1, rows, :] * (mul(high, earlier) + mul(low, earlier))
        high, low = parts(swell[2, rows, :] * (temp - before), 2)
        flux[0, to, :] = high
        flux[1, to, :] = low
    own = hit[:, part * slots : (part + 1) * slots]
    total = mul(own, flux[0]) + mul(own, flux[1])
    for other in earlier_sink:
        total = total + other[...]
    sink[...] = total


def conduct_kernel(
    old, heat, west, east, sink, solid, cols, sems
):
    del old
    nz, nx, ny = heat.shape
    del sems
    inner = pl.ds(0, nx)
    lot, n_span = lax.axis_index("span"), lax.axis_size("span")
    lane = iota((nx, ny), 1)
    sub = iota((nx, ny), 0)
    border = (lane == 0) | (lane == ny - 1)
    ends = jnp.where(lane < nz, 0, ny - 1)
    halo = jnp.where((lane < nz) & (lot < n_span - 1), east[...], 0.0)
    halo = jnp.where((lane >= nz) & (lot > 0), west[...], halo)
    unroll = 4

    def some(i, state):
        found, low = state
        for j in range(unroll):
            z = i * unroll + j
            mid = solid[z + 1, inner, :]
            side = pick(halo, jnp.where(lane == 0, nz, 0) + z)
            right, left = pltpu.roll(mid, 1, 1), pltpu.roll(mid, ny - 1, 1)
            across = jnp.where(border, side + jnp.where(lane == 0, left, right), left + right)
            above = jnp.where(sub == 0, 0.0, pltpu.roll(mid, 1, 0))
            below = jnp.where(sub == nx - 1, 0.0, pltpu.roll(mid, nx - 1, 0))
            total = across + (above + below)
            total = total + (low + solid[z + 2, inner, :])
            new = mid + KAPPA * (total - 6.0 * mid) + heat[z]
            solid[z + 1, inner, :] = new
            found = jnp.where(lane % nz == z, pick(new, ends), found)
            low = mid
        return found, low

    zero = jnp.zeros((nx, ny), F32)
    cols[...], _ = lax.fori_loop(0, nz // unroll, some, (zero, zero))
    solid[1, inner, :] = solid[1, inner, :] - sink[...]


def entering(got, scan):
    n_flow = got.shape[0]
    ends = [[], []]
    for g in range(n_flow // TILE):
        rows = slice(g * TILE, (g + 1) * TILE)
        lanes = [scan[12, half, rows, :].astype(I32) for half in range(2)]
        origin = [scan[13, half, rows, :] for half in range(2)]
        acc = [jnp.zeros((TILE, LANES), F32) for _ in range(2)]
        for o in range(n_flow):
            line = jnp.broadcast_to(got[o, g : g + 1, :], (TILE, LANES))
            for half in range(2):
                acc[half] = jnp.where(origin[half] == float(o), pick(line, lanes[half]), acc[half])
        for half in range(2):
            ends[half].append(acc[half])
    result = []
    sub, lane = iota((n_flow, LANES), 0), iota((n_flow, LANES), 1)
    for half in range(2):
        x = jnp.concatenate(ends[half], axis=0)
        for step in range(4):
            x = x + scan[step, half] * pltpu.roll(x, 1 << step, 1)
        inlet = scan[11, half]
        y = jnp.where(sub == 0, x + scan[9, half] * inlet, x)
        for step in range(5):
            y = y + scan[4 + step, half] * pltpu.roll(y, 1 << step, 0)
        carry = jnp.where(sub == 0, inlet, pltpu.roll(y, 1, 0))
        carry = pick(carry, lane // 16 * 16 + 15)
        earlier = jnp.where(lane % 16 == 0, 0.0, pltpu.roll(x, 1, 1))
        result.append(earlier + scan[10, half] * carry)
    return result


def hosted(enter, scan):
    lane8, sub8 = iota((TILE, LANES), 1), iota((TILE, LANES), 0)
    found = []
    for g in range(enter[0].shape[0] // TILE):
        rows = slice(g * TILE, (g + 1) * TILE)
        seg = scan[14, 0, rows, :].astype(I32)
        low, high = (pick(enter[half][rows], seg % LANES) for half in range(2))
        value = jnp.where(lane8 // SLOTS == sub8, jnp.where(seg < LANES, low, high), 0.0)
        found.append(jnp.sum(value, axis=0, keepdims=True))
    return jnp.concatenate(found, axis=1)


def new_bottom(carry, base, hit, reply):
    high, low = parts(carry, 2)
    high, low = hit * high, hit * low
    return base + (mul(high, reply[0]) + (mul(high, reply[1]) + mul(low, reply[0])))


def after_kernel(
    last,
    got, old, plain, scan, hit, reply_hbm, weight_hbm, hit_t,
    solid, msg_hbm, cols,
    edges, msg, reply, weight, sems,
):
    del old
    copies = Copies(sems)
    come = [copies.start(reply_hbm, reply), copies.start(weight_hbm, weight)]
    carry = hosted(entering(got, scan), scan)
    own_hit = hit[...]
    nx = own_hit.shape[0]
    inner = pl.ds(0, nx)
    north, south = add_outer_rows(solid, got)
    come[0].wait()
    new = new_bottom(carry, solid[1, inner, :], own_hit, reply)
    solid[1, inner, :] = new
    come[1].wait()
    write_shifts(new, weight, own_hit.astype(F32), msg)
    back = send_message(copies, solid, msg, edges, msg_hbm)
    nx, ny = new.shape
    nz = edges.shape[1]
    if last:
        padded = jnp.concatenate([new, jnp.zeros((LANES - nx, ny), F32)], axis=0)
        temp = sum(mul(hit_t[...], part) for part in parts(padded, 3))
        for p in range(msg.shape[0]):
            msg[p, TILE : TILE + SLOTS, :] = temp[p * SLOTS : (p + 1) * SLOTS]
        rows = pl.ds(TILE + nz, SLOTS)
        back.append(copies.start(msg.at[:, pl.ds(TILE, SLOTS), :], msg_hbm.at[:, rows, :]))
    sub, lane = iota((nx, ny), 0), iota((nx, ny), 1)
    sub_z, lane_z = iota((nz, ny), 0), iota((nz, ny), 1)

    def ends_of(rows):
        both = jnp.where(lane_z < nz, rows[:, 0:1], rows[:, ny - 1 : ny])
        both = jnp.where((lane_z % nz == sub_z) & (lane_z < 2 * nz), both, 0.0)
        return jnp.sum(both, axis=0, keepdims=True)

    value = plain[...] + jnp.where(sub == 0, ends_of(north), 0.0)
    value = value + jnp.where(sub == nx - 1, ends_of(south), 0.0)
    cols[...] = jnp.where(lane % nz == 0, pick(new, jnp.where(lane < nz, 0, ny - 1)), value)
    for copy in back:
        copy.wait()


def final_kernel(
    got, old, place_hbm, cond_hbm, scan, hit, reply_hbm, solid, out_hbm, coolant_hbm,
    place, cond, reply, coolant, sems,
):
    copies = Copies(sems)
    nz, nx = out_hbm.shape[0], out_hbm.shape[1]
    inner = pl.ds(0, nx)
    del old
    come = copies.start(reply_hbm, reply)
    then = [copies.start(place_hbm, place), *load_segments(copies, cond_hbm, cond)]
    add_outer_rows(solid, got)
    upper = pl.ds(2, nz - 1)
    back = [copies.start(solid.at[upper, inner, :], out_hbm.at[pl.ds(1, nz - 1)])]
    enter = entering(got, scan)
    carry = hosted(enter, scan)
    come.wait()
    solid[1, inner, :] = new_bottom(carry, solid[1, inner, :], hit[...], reply)
    back.append(copies.start(solid.at[1, inner, :], out_hbm.at[0]))
    for copy in then:
        copy.wait()
    n_flow = got.shape[0]
    stacked = got[:, TILE + nz :, :].reshape(n_flow * SLOTS, LANES)
    temp = sum(mul(place[...], part) for part in parts(stacked, 3))
    segs = temp.shape[0]
    lane = iota((segs, LANES), 1)
    gain = jnp.exp(-cond[...].reshape(segs, LANES))
    shift = (1.0 - gain) * temp
    for step in range(7):
        width = 1 << step
        shift = shift + jnp.where(lane >= width, gain * pltpu.roll(shift, width, 1), 0.0)
        gain = gain * jnp.where(lane >= width, pltpu.roll(gain, width, 1), 1.0)
    own = iota((n_flow, LANES), 0) == lax.axis_index("flow")
    line = jnp.concatenate(
        [jnp.sum(jnp.where(own, part, 0.0), axis=0, keepdims=True) for part in enter], axis=1
    )
    same = iota((segs, segs), 0) == iota((segs, segs), 1)
    start = jnp.sum(jnp.where(same, line, 0.0), axis=1, keepdims=True)
    coolant[...] = (shift + gain * start).reshape(coolant.shape)
    for s in range(coolant.shape[1]):
        target = coolant_hbm.at[:, pl.ds(s * LANES, LANES)]
        back.append(copies.start(coolant.at[:, s, :], target))
    for copy in back:
        copy.wait()


def body(solid_start, heat_gen, conductance, heat_capacity, inlet_temp, wall_owner, wall_row):
    n_flow, n_span = lax.axis_size("flow"), lax.axis_size("span")
    nz, nx, ny = solid_start.shape
    channels, stations = conductance.shape
    segs = wall_owner.shape[0]
    slots = n_flow * SLOTS
    const = jnp.pad(
        jnp.stack([heat_capacity, inlet_temp]), ((0, TILE - 2), (0, LANES - channels))
    )

    def exchange(message):
        return lax.all_to_all(message, "flow", 0, 0, tiled=True)

    lines = spec((segs // LANES, LANES), I32)
    split = spec((channels, segs // channels, LANES))
    layer, edges_spec = spec((nx, ny)), spec((2, nz, ny))
    block = spec((nz, nx, ny))
    pay_spec, place_spec = spec((n_flow, SLOTS + TILE, LANES)), spec((segs, slots), BF16)
    pay, place = call(
        source_kernel,
        (wall_owner.reshape(lines.shape), wall_row.reshape(lines.shape), conductance),
        (pay_spec, place_spec),
        (lines, lines, split, pay_spec, place_spec),
        20,
        limit=WHOLE_VMEM,
    )
    got = exchange(pay)
    room = spec((nz + 2, nx, ny))
    solid, cols = call(
        outer_kernel, (solid_start,), (room, layer), (), 1, held_out=(0, 1), limit=WHOLE_VMEM
    )
    hit_spec, hit_t_spec = spec((nx, slots), BF16), spec((slots, LANES), BF16)
    reply_spec, weight_spec = spec((2, slots, LANES), BF16), spec((2, LANES, slots), BF16)
    swell_spec = spec((3, slots, LANES))
    scan_spec = spec((15, 2, n_flow, LANES))
    msg_spec = spec((n_flow, TILE + nz, LANES))
    long_spec = spec((n_flow, TILE + nz + SLOTS, LANES))
    short_spec = spec((n_flow, TILE, LANES))
    constants = (
        hit_spec, hit_t_spec, reply_spec, weight_spec, swell_spec, scan_spec, msg_spec,
    )
    hit, hit_t, reply, weight, swell, scan, message = call(
        owner_kernel,
        (got, solid, const),
        constants,
        (pay_spec, spec((TILE, LANES)), short_spec, edges_spec),
        5,
        held=(1,),
        held_out=range(6),
    )

    def march(part, *operands):
        (sink,) = call(
            functools.partial(march_kernel, part),
            operands,
            (layer,),
            (spec((2, slots // 2, LANES), BF16),),
            1,
            held=range(len(operands)),
            held_out=(0,),
            flops=1_000_000,
            nbytes=1_500_000,
        )
        return sink

    def beside(solid, cols, message):
        got = exchange(message)
        up = [(i, (i + 1) % n_span) for i in range(n_span)]
        down = [(i, (i - 1) % n_span) for i in range(n_span)]
        west = lax.ppermute(cols, "span", up)
        sink = march(0, solid, hit, hit_t, swell)
        cols, sink = lax.optimization_barrier((cols, sink))
        east = lax.ppermute(cols, "span", down)
        west, sink = lax.optimization_barrier((west, sink))
        sink = march(1, solid, hit, hit_t, swell, sink)
        solid, cols = call(
            conduct_kernel,
            (solid, heat_gen, west, east, sink),
            (room, layer),
            (),
            1,
            held=range(5),
            held_out=(0, 1),
            flops=4_000_000,
            nbytes=6_000_000,
            aliases={0: 0},
        )
        return got, solid, cols

    def step(state, last=False):
        got, solid, cols = beside(*state)
        solid, message, cols = call(
            functools.partial(after_kernel, last),
            (got, solid, cols, scan, hit, reply, weight, hit_t),
            (room, long_spec if last else msg_spec, layer),
            (
                edges_spec, spec((n_flow, TILE + SLOTS, LANES)) if last else short_spec,
                reply_spec, weight_spec,
            ),
            6,
            held=(0, 1, 2, 3, 4, 7),
            held_out=(0, 2),
            flops=4_000_000,
            nbytes=4_000_000,
            aliases={1: 0},
        )
        return solid, cols, message

    state = lax.fori_loop(0, STEPS - 2, lambda turn, now: step(now), (solid, cols, message))
    got, solid, _ = beside(*step(state, last=True))
    _, solid, coolant = call(
        final_kernel,
        (got, solid, place, conductance, scan, hit, reply),
        (room, block, spec((channels, stations))),
        (place_spec, split, reply_spec, split),
        4 + 2 * split.shape[1],
        held=(0, 1, 4, 5),
        held_out=(0,),
        aliases={1: 0},
    )
    return solid, coolant


def solution(mesh):
    placed = (
        P(None, "flow", "span"),
        P(None, "flow", "span"),
        P("span", "flow"),
        P("span"),
        P("span"),
        P(("flow", "span"), None),
        P(("flow", "span"), None),
    )
    return jax.shard_map(
        body,
        mesh=mesh,
        in_specs=placed,
        out_specs=(P(None, "flow", "span"), P("span", "flow")),
        check_vma=False,
    )
```
